128 devices in a mesh: wide: 32 (over z, y, x_hi), narrow: 4 (over x_lo, core).
Axes of the slice: x: 4 (x_hi: 2, x_lo: 2; x = x_hi * 2 + x_lo), y: 4, z: 4, core: 2. Of those that a mesh axis runs over, the one named last changes fastest.
Arguments:
- control: bfloat16 [512, 2, 512, 512], P('wide', None, None, 'narrow'), may hold values from -6 to 6
- legendre: bfloat16 [512, 512, 512], P('wide'), may hold values from -0.25 to 0.25
- loc_spectrum: float32 [512, 512], P('wide'), may hold values from 0.02 to 0.2
- ensemble: bfloat16 [512, 512, 1024], P('wide', 'narrow'), may hold values from -0.29882812 to 0.29882812
- order_map: int32 [512], replicated, may hold values from 0 to 511, each once
- obs_level: int32 [512, 256], P('wide'), may hold values from 0 to 7
- obs_lon: int32 [512, 256], P('wide'), may hold values from 0 to 1023
- obs_value: float32 [512, 256], P('wide'), may hold values from -12 to 12
- obs_weight: float32 [512, 256], P('wide'), may hold values from 2 to 40
Outputs:
- gradient: float32 [512, 2, 512, 512], P('wide', None, None, 'narrow')
The draws below stay inside these ranges and needn't reach their ends.
Inputs may be any that keep to these rules, and one draw needn't show every extreme that they name: order_map is a permutation of the orders 0 to 511. `obs_lon`: several observations may share a grid point.
All inputs are finite; a program needn't handle non-finite values.
Results may differ from the reference program's by a relative error of at most 0.0057.
Values may be sent and summed in bfloat16 or wider, within the bound.
No kernel may reach another device: no remote copies, remote signals or barrier semaphores. Data moves between devices by JAX's collectives and lax.ppermute only.
A program may use at most 128 MiB of HBM per device.

```python
import math
import jax
import jax.numpy as jnp
from jax import lax

M = 512
NDEG = 512
NLAT = 512
NLON = 1024
K = 64
LEVELS = 8
NOBS = 256


def place_ends(entries, rng, low, high):
    spot = [jax.random.randint(jax.random.fold_in(rng, axis), (), 0, length) for axis, length in enumerate(entries.shape)]
    widest = entries.shape.index(max(entries.shape))
    beside = spot[:widest] + [(spot[widest] + 1) % entries.shape[widest]] + spot[widest + 1:]
    return entries.at[tuple(spot)].set(low).at[tuple(beside)].set(high)


def level_of(key, dims, shards, low, largest):
    def one(position, parts):
        draws = jax.random.uniform(jax.random.fold_in(jax.random.fold_in(key, 6), position), (parts,), jnp.float32, low / len(shards), largest / len(shards))
        return jnp.repeat(jnp.exp(draws), dims[position] // parts).reshape((-1,) + (1,) * (len(dims) - position - 1))

    level = one(*shards[0])
    for cut in shards[1:]:
        level = level * one(*cut)
    return level


def scatter_about(key, shape, deviation, reach, split=(), kind=jnp.bfloat16):
    entries = jax.random.normal(key, shape, jnp.float32) * deviation
    if len(split) > 0:
        entries = level_of(key, shape, split, -0.22, 0.18) * entries
    return jnp.clip(entries, min=-reach, max=reach).astype(kind)


def setup_inputs(seed: int = 0) -> dict:
    key_of = jax.random.split(jax.random.key(seed), 10)
    control = scatter_about(key_of[0], (M, 2, NDEG, K * LEVELS), 1.0, 6.0, ((0, 32), (3, 4)))
    legendre = scatter_about(key_of[1], (M, NDEG, NLAT), NDEG ** -0.5, 0.25, ((0, 32),))
    loc_spectrum = jnp.clip(jnp.exp(math.log(0.2) - 2.3025851 * jax.random.uniform(key_of[2], (M, NDEG), jnp.float32) ** level_of(key_of[2], (M, NDEG), ((0, 32),), -0.2, 0.2)), 0.02, 0.2)
    ensemble = scatter_about(key_of[3], (NLAT, K * LEVELS, NLON), 0.05, 0.29882812, ((0, 32), (1, 4)))
    order_map = jax.random.permutation(key_of[4], M).astype(jnp.int32)
    obs_level = place_ends(jax.random.randint(key_of[5], (NLAT, NOBS), 0, LEVELS), jax.random.fold_in(key_of[5], 1), 0, LEVELS - 1).astype(jnp.int32)
    obs_lon = place_ends(jax.random.randint(key_of[6], (NLAT, NOBS), 0, NLON), jax.random.fold_in(key_of[6], 1), 0, NLON - 1).astype(jnp.int32)
    obs_value = scatter_about(key_of[7], (NLAT, NOBS), 2.0, 12.0, ((0, 32),), jnp.float32)
    obs_weight = jnp.clip(jnp.exp(math.log(40.0) - 2.9957323 * jax.random.uniform(key_of[8], (NLAT, NOBS), jnp.float32) ** level_of(key_of[8], (NLAT, NOBS), ((0, 32),), -0.2, 0.2)), 2.0, 40.0)
    return dict(control=control, legendre=legendre, loc_spectrum=loc_spectrum, ensemble=ensemble, order_map=order_map, obs_level=obs_level, obs_lon=obs_lon, obs_value=obs_value, obs_weight=obs_weight)


def fourier_table(order_map, count):
    longitude = jnp.arange(count, dtype=jnp.int32)
    turns = (order_map[:, None] * longitude[None, :]) % count
    angle = turns.astype(jnp.float32) * (2.0 * math.pi / count)
    factor = jnp.where(order_map == 0, 1.0, 2.0).astype(jnp.float32)[:, None]
    return jnp.stack([factor * jnp.cos(angle), -factor * jnp.sin(angle)], axis=1)


def reference(control, legendre, loc_spectrum, ensemble, order_map, obs_level, obs_lon, obs_value, obs_weight):
    column_count = K * LEVELS
    scaled = (control.astype(jnp.float32) * loc_spectrum[:, None, :, None]).astype(jnp.bfloat16)

    def legendre_slot(pair):
        values_m, coeff_m = pair
        flat_coeff = coeff_m.transpose(1, 0, 2).reshape(NDEG, 2 * column_count)
        return jnp.dot(values_m.T, flat_coeff, preferred_element_type=jnp.float32).astype(jnp.bfloat16)

    coeff = lax.map(legendre_slot, (legendre, scaled))
    coeff = coeff.reshape(M, NLAT, 2, column_count).transpose(1, 0, 2, 3).reshape(NLAT, 2 * M, column_count)
    fourier = fourier_table(order_map, NLON).reshape(2 * M, NLON).astype(jnp.bfloat16)

    def row_work(inputs):
        coeff_row, ens_row, level_row, lon_row, value_row, weight_row = inputs
        field = jnp.dot(coeff_row.T, fourier, preferred_element_type=jnp.float32)
        ens_full = ens_row.astype(jnp.float32).reshape(K, LEVELS, NLON)
        increment = jnp.sum(field.reshape(K, LEVELS, NLON) * ens_full, axis=0)
        flat_index = level_row * NLON + lon_row
        picked = increment.reshape(-1)[flat_index]
        misfit = weight_row * (picked - value_row)
        obs_grad = jnp.zeros((LEVELS * NLON,), jnp.float32).at[flat_index].add(misfit).reshape(LEVELS, NLON)
        member_grad = (obs_grad[None] * ens_full).reshape(column_count, NLON).astype(jnp.bfloat16)
        return jnp.dot(fourier, member_grad.T, preferred_element_type=jnp.float32).astype(jnp.bfloat16)

    backward = lax.map(row_work, (coeff, ensemble, obs_level, obs_lon, obs_value, obs_weight))
    backward = backward.reshape(NLAT, M, 2 * column_count).transpose(1, 0, 2)

    def adjoint_slot(pair):
        values_m, back_m = pair
        summed = jnp.dot(values_m, back_m, preferred_element_type=jnp.float32)
        return summed.reshape(NDEG, 2, column_count).transpose(1, 0, 2)

    adjoint = lax.map(adjoint_slot, (legendre, backward))
    return control.astype(jnp.float32) + loc_spectrum[:, None, :, None] * adjoint
```

```python
import jax
import jax.numpy as jnp
from jax import lax
from jax.experimental import pallas as pl
from jax.experimental.pallas import tpu as pltpu
from jax.sharding import PartitionSpec as P

LEVELS = 8
ROWS = 16
PLANES = 18
SIN = (6.2831851595779975, -41.34165492085311, 81.60099762205961, -76.54964290998956, 39.53570242643394)
COS = (0.9999999532360554, -19.739171315085017, 64.93458093602055, -85.24007915837501, 56.24034662339592)


def params(mib):
    return pltpu.CompilerParams(vmem_limit_bytes=mib * 2**20)


def horner(coefs, x):
    total = jnp.full_like(x, coefs[-1])
    for c in coefs[-2::-1]:
        total = total * x + c
    return total


def pick_kernel(level_ref, lon_ref, ens_ref, out_ref):
    b = pl.program_id(0)

    @pl.when(b == 0)
    def _():
        lon = lon_ref[...]
        out_ref[16] = (lon >> 3).astype(jnp.float32).astype(jnp.bfloat16)
        out_ref[17] = ((lon & 7) * LEVELS + level_ref[...]).astype(jnp.float32).astype(jnp.bfloat16)

    lon = lon_ref[pl.ds(b, 1), :]
    level = level_ref[pl.ds(b, 1), :]
    members, nobs = out_ref.shape[1], out_ref.shape[2]
    lons = ens_ref.shape[2]
    step = 256
    total = jnp.zeros((ens_ref.shape[1], nobs), jnp.float32)
    place = lax.broadcasted_iota(jnp.int32, (step, nobs), 0)
    for s in range(0, lons, step):
        onehot = jnp.where(place == lon - s, 1.0, 0.0).astype(jnp.bfloat16)
        total += jnp.dot(ens_ref[0, :, s : s + step], onehot, preferred_element_type=jnp.float32)
    mine = lax.broadcasted_iota(jnp.int32, (LEVELS, nobs), 0) == level
    total = jnp.where(mine[None], total.reshape(members, LEVELS, nobs), 0.0)
    out_ref[b] = jnp.sum(total, axis=1).astype(jnp.bfloat16)


def pick(obs_level, obs_lon, ensemble):
    rows, width, lons = ensemble.shape
    nobs = obs_lon.shape[1]
    whole = pl.BlockSpec((rows, nobs), lambda b: (0, 0))
    return pl.pallas_call(
        pick_kernel,
        grid=(rows,),
        in_specs=[whole, whole, pl.BlockSpec((1, width, lons), lambda b: (b, 0, 0))],
        out_specs=pl.BlockSpec((PLANES, rows, nobs), lambda b: (0, 0, 0)),
        out_shape=jax.ShapeDtypeStruct((PLANES, rows, nobs), jnp.bfloat16),
        compiler_params=params(32),
        name="pick",
    )(obs_level, obs_lon, ensemble)


def column(loc_ref, m):
    row = loc_ref[pl.ds(m, 1), :]
    return jnp.broadcast_to(row, (128, row.shape[1])).T


def legendre_kernel(leg_ref, control_ref, loc_ref, out_ref, acc_ref):
    m = pl.program_id(0)
    slots = pl.num_programs(0)
    lats = out_ref.shape[0]
    width = control_ref.shape[3]
    loc = column(loc_ref, m)
    scaled = [
        (control_ref[0, c].astype(jnp.float32) * loc).astype(jnp.bfloat16) for c in range(2)
    ]
    got = lax.dot_general(
        leg_ref[0],
        jnp.concatenate(scaled, axis=1),
        (((0,), (0,)), ((), ())),
        preferred_element_type=jnp.float32,
    )
    for c in range(2):
        acc_ref[pl.ds(c * ROWS + m, lats, stride=2 * ROWS), :] = got[:, c * width : (c + 1) * width]

    @pl.when(m == slots - 1)
    def _():
        for s in range(0, lats, 64):
            out_ref[s : s + 64] = (
                acc_ref[s * 2 * ROWS : (s + 64) * 2 * ROWS, :]
                .reshape(64, 2 * ROWS, width)
                .astype(jnp.bfloat16)
            )


def legendre_forward(legendre, control, loc):
    slots, _, degs, width = control.shape
    lats = legendre.shape[2]
    return pl.pallas_call(
        legendre_kernel,
        grid=(slots,),
        in_specs=[
            pl.BlockSpec((1, degs, lats), lambda m: (m, 0, 0)),
            pl.BlockSpec((1, 2, degs, width), lambda m: (m, 0, 0, 0)),
            pl.BlockSpec((slots, degs), lambda m: (0, 0)),
        ],
        out_specs=pl.BlockSpec((lats, 2 * slots, width), lambda m: (0, 0, 0)),
        out_shape=jax.ShapeDtypeStruct((lats, 2 * slots, width), jnp.bfloat16),
        scratch_shapes=[pltpu.VMEM((lats * 2 * slots, width), jnp.float32)],
        compiler_params=params(40),
        cost_estimate=pl.CostEstimate(
            flops=2 * slots * degs * lats * 2 * width, bytes_accessed=16 * 2**20, transcendentals=0
        ),
        name="legendre_forward",
    )(legendre, control, loc)


def forward_kernel(ids_ref, e_ref, coeff_ref, order_ref, factor_ref, *rest):
    part_ref, four_ref, keep_ref, lon_ref, lev_ref = rest[-5:]
    hi = e_ref[0, 16].astype(jnp.float32)
    lo = e_ref[0, 17].astype(jnp.float32)
    low = jnp.floor(lo * (1.0 / LEVELS))
    lon_ref[...] = hi * 8.0 + low
    lev_ref[...] = lo - low * LEVELS
    keep_ref[0] = e_ref[0]
    order = order_ref[...]
    factor = factor_ref[...]
    nobs = e_ref.shape[3]
    members = e_ref.shape[2]
    grid_level = lax.broadcasted_iota(jnp.int32, (LEVELS, nobs), 0).astype(jnp.float32)

    def one(b):
        turns = order * lon_ref[pl.ds(b, 1), :] * (1.0 / 1024.0)
        frac = turns - jnp.floor(turns + 0.5)
        fold = 0.25 - jnp.abs(frac)
        square = fold * fold
        cosine = factor * (fold * horner(SIN, square))
        sine = jnp.where(frac < 0.0, factor, -factor) * horner(COS, square)
        four = jnp.concatenate([cosine.astype(jnp.bfloat16), sine.astype(jnp.bfloat16)], axis=0)
        four_ref[0, b] = four
        field = lax.dot_general(
            coeff_ref[b], four, (((0,), (0,)), ((), ())), preferred_element_type=jnp.float32
        )
        ens = e_ref[0, b].astype(jnp.float32)
        field = field.reshape(members, LEVELS, nobs) * ens[:, None, :]
        field = jnp.sum(field, axis=0)
        mine = grid_level == lev_ref[pl.ds(b, 1), :]
        part_ref[pl.ds(b, 1), :] = jnp.sum(jnp.where(mine, field, 0.0), axis=0, keepdims=True)

    def some(i, carry):
        for k in range(4):
            one(i * 4 + k)
        return carry

    lax.fori_loop(0, ROWS // 4, some, 0)


def forward(ids, e, coeff, order, factor, before):
    n = e.shape[0]
    lats, modes, width = coeff.shape
    nobs = e.shape[3]
    blocks = lats // ROWS
    whole = pl.BlockSpec(order.shape, lambda i, ids: (0, 0))
    e_spec = lambda f: pl.BlockSpec((1, PLANES, ROWS, nobs), f)
    at_ids = lambda i, ids: (ids[i], 0, 0, 0)
    out_shape = (
        jax.ShapeDtypeStruct((lats, nobs), jnp.float32),
        jax.ShapeDtypeStruct((blocks, ROWS, modes, nobs), jnp.bfloat16),
        jax.ShapeDtypeStruct((blocks, PLANES, ROWS, nobs), jnp.bfloat16),
    )
    passed = () if before is None else tuple(before)
    return pl.pallas_call(
        forward_kernel,
        grid_spec=pltpu.PrefetchScalarGridSpec(
            num_scalar_prefetch=1,
            grid=(n,),
            in_specs=[
                e_spec(lambda i, ids: (i, 0, 0, 0)),
                pl.BlockSpec((ROWS, modes, width), lambda i, ids: (ids[i], 0, 0)),
                whole,
                whole,
            ]
            + [pl.BlockSpec(memory_space=pl.ANY)] * len(passed),
            out_specs=(
                pl.BlockSpec((ROWS, nobs), lambda i, ids: (ids[i], 0)),
                pl.BlockSpec((1, ROWS, modes, nobs), at_ids),
                e_spec(at_ids),
            ),
            scratch_shapes=[pltpu.VMEM((ROWS, nobs), jnp.float32)] * 2,
        ),
        out_shape=out_shape,
        input_output_aliases={5 + i: i for i in range(len(passed))},
        compiler_params=params(16),
        cost_estimate=pl.CostEstimate(
            flops=n * 2 * 10**9, bytes_accessed=n * 2**20, transcendentals=0
        ),
        name="observe",
    )(ids, e, coeff, order, factor, *passed)


def backward_kernel(
    e_ref, four_ref, misfit_ref, leg_ref, control_ref, loc_ref, out_ref, back_ref, lev_ref
):
    step = pl.program_id(0)
    blocks = misfit_ref.shape[0] // ROWS
    nobs = misfit_ref.shape[1]
    members = e_ref.shape[2]
    modes = four_ref.shape[2]
    lats = misfit_ref.shape[0]
    width = control_ref.shape[3]

    @pl.when(step < blocks)
    def _():
        lo = e_ref[0, 17].astype(jnp.float32)
        lev_ref[...] = lo - jnp.floor(lo * (1.0 / LEVELS)) * LEVELS
        grid_level = lax.broadcasted_iota(jnp.int32, (LEVELS, nobs), 0).astype(jnp.float32)

        def one(b):
            row = step * ROWS + b
            ens = e_ref[0, b].astype(jnp.float32) * misfit_ref[pl.ds(row, 1), :]
            mine = grid_level == lev_ref[pl.ds(b, 1), :]
            spread = jnp.where(mine[None], ens[:, None, :], 0.0)
            spread = spread.reshape(members * LEVELS, nobs).astype(jnp.bfloat16)
            back_ref[pl.ds(pl.multiple_of(row * modes, modes), modes), :] = lax.dot_general(
                four_ref[0, b],
                spread,
                (((1,), (1,)), ((), ())),
                preferred_element_type=jnp.float32,
            )

        def some(i, carry):
            for k in range(4):
                one(i * 4 + k)
            return carry

        lax.fori_loop(0, ROWS // 4, some, 0)

    @pl.when(step >= blocks)
    def _():
        m = step - blocks
        pieces = [
            back_ref[pl.ds(c * ROWS + m, lats, stride=modes), :].astype(jnp.bfloat16)
            for c in range(2)
        ]
        got = jnp.dot(
            leg_ref[0], jnp.concatenate(pieces, axis=1), preferred_element_type=jnp.float32
        )
        loc = column(loc_ref, m)
        for c in range(2):
            out_ref[0, c] = (
                control_ref[0, c].astype(jnp.float32) + loc * got[:, c * width : (c + 1) * width]
            )


def backward(e, four, misfit, legendre, control, loc):
    blocks, _, _, nobs = e.shape
    modes = four.shape[2]
    slots, _, degs, width = control.shape
    lats = legendre.shape[2]
    first = lambda s: jnp.minimum(s, blocks - 1)
    second = lambda s: jnp.maximum(s - blocks, 0)
    per_slot = pl.BlockSpec((1, 2, degs, width), lambda s: (second(s), 0, 0, 0))
    return pl.pallas_call(
        backward_kernel,
        grid=(blocks + slots,),
        in_specs=[
            pl.BlockSpec((1, PLANES, ROWS, nobs), lambda s: (first(s), 0, 0, 0)),
            pl.BlockSpec((1, ROWS, modes, nobs), lambda s: (first(s), 0, 0, 0)),
            pl.BlockSpec((lats, nobs), lambda s: (0, 0)),
            pl.BlockSpec((1, degs, lats), lambda s: (second(s), 0, 0)),
            per_slot,
            pl.BlockSpec((slots, degs), lambda s: (0, 0)),
        ],
        out_specs=per_slot,
        out_shape=jax.ShapeDtypeStruct(control.shape, jnp.float32),
        scratch_shapes=[
            pltpu.VMEM((lats * modes, width), jnp.float32),
            pltpu.VMEM((ROWS, nobs), jnp.float32),
        ],
        compiler_params=params(40),
        name="adjoint",
    )(e, four, misfit, legendre, control, loc)


def shift(x, dz=0, dy=0, dx=0):
    pairs = []
    for w in range(32):
        z, y, h = w // 8, w // 2 % 4, w % 2
        pairs.append((w, (z + dz) % 4 * 8 + (y + dy) % 4 * 2 + (h + dx) % 2))
    return lax.ppermute(x, "wide", pairs)


def body(
    control, legendre, loc_spectrum, ensemble, order_map, obs_level, obs_lon, obs_value, obs_weight
):
    slots, _, _, width = control.shape
    nobs = obs_lon.shape[1]
    both = ("wide", "narrow")
    w = lax.axis_index("wide")
    n = lax.axis_index("narrow")
    z, y, h = w // 8, w // 2 % 4, w % 2

    def place(dz, dy, dx=0):
        return (z + dz) % 4 * 8 + (y + dy) % 4 * 2 + (h + dx) % 2

    order = lax.dynamic_slice(order_map, (w * slots,), (slots,))
    factor = jnp.where(order == 0, 1.0, 2.0).astype(jnp.float32)
    order = jnp.broadcast_to(order.astype(jnp.float32)[:, None], (slots, nobs))
    factor = jnp.broadcast_to(factor[:, None], (slots, nobs))

    own = pick(obs_level, obs_lon, ensemble)

    half = PLANES // 2

    def ring4(x, cut, **axis):
        (name, _), = axis.items()
        one = shift(x, **{name: 1})
        three = shift(x, **{name: -1})
        two = (shift(one[:cut], **{name: 1}), shift(three[cut:], **{name: -1}))
        return one, two, three

    other = shift(own, dx=1)
    a1, a2, a3 = ring4(own, half, dy=1)
    a = jnp.concatenate([own, a1, *a2, a3], axis=0)
    x1, x2, x3 = ring4(other, half, dz=1)
    x = jnp.concatenate([other, x1, *x2, x3], axis=0)
    az1, az2, az3 = ring4(a, 2 * PLANES, dz=1)
    xy1, xy2, xy3 = ring4(x, 2 * PLANES, dy=1)

    steps = (0, -1, -2, 1)
    a_ids = lambda dz: [place(dz, s) for s in steps]
    x_ids = lambda dy: [place(s, dy, 1) for s in steps]
    far = lambda t: jnp.concatenate(t, axis=0)
    chunks = [
        (a, a_ids(0)),
        (x, x_ids(0)),
        (az1, a_ids(-1)),
        (az3, a_ids(1)),
        (xy1, x_ids(-1)),
        (xy3, x_ids(1)),
        (far(az2), a_ids(-2)),
        (far(xy2), x_ids(-2)),
    ]
    coeff = legendre_forward(legendre, control, loc_spectrum)
    state = None
    for e, ids in chunks:
        e = e.reshape(-1, PLANES, ROWS, nobs)
        state = forward(jnp.stack(ids).astype(jnp.int32), e, coeff, order, factor, state)
    part, four, e_all = state

    devices = lax.axis_size(both)
    mine = part.shape[0] // devices
    parts = lax.all_to_all(part, both, split_axis=0, concat_axis=0, tiled=True)
    picked = jnp.sum(parts.reshape(devices, mine, nobs), axis=0)
    value = lax.dynamic_slice_in_dim(obs_value, n * mine, mine, 0)
    weight = lax.dynamic_slice_in_dim(obs_weight, n * mine, mine, 0)
    misfit = weight * (picked - value)
    misfit = jnp.broadcast_to(misfit[None], (devices, mine, nobs)).reshape(part.shape)
    misfit = lax.all_to_all(misfit, both, split_axis=0, concat_axis=0, tiled=True)
    return backward(e_all, four, misfit, legendre, control, loc_spectrum)


def solution(mesh):
    rows = P("wide", None)
    return jax.shard_map(
        body,
        mesh=mesh,
        in_specs=(
            P("wide", None, None, "narrow"),
            P("wide", None, None),
            rows,
            P("wide", "narrow", None),
            P(),
            rows,
            rows,
            rows,
            rows,
        ),
        out_specs=P("wide", None, None, "narrow"),
        check_vma=False,
    )
```

```python
import jax
import jax.numpy as jnp
from jax import lax
from jax.experimental import pallas as pl
from jax.experimental.pallas import tpu as pltpu
from jax.sharding import PartitionSpec as P

LEVELS = 8
ROWS = 16
PLANES = 18
PITCH = 33
SIN = (6.2831851595779975, -41.34165492085311, 81.60099762205961, -76.54964290998956, 39.53570242643394)
COS = (0.9999999532360554, -19.739171315085017, 64.93458093602055, -85.24007915837501, 56.24034662339592)
HALF_SIN = tuple(2**0.5 * c / 2 ** (2 * i + 1) for i, c in enumerate(SIN))
HALF_COS = tuple(-(2**0.5) * c / 4**i for i, c in enumerate(COS))


def params():
    return pltpu.CompilerParams(vmem_limit_bytes=63 * 2**20)


def horner(coefs, x):
    total = jnp.full_like(x, coefs[-1])
    for c in coefs[-2::-1]:
        total = total * x + c
    return total


def pick_kernel(level_ref, lon_ref, ens_ref, out_ref):
    b = pl.program_id(0)

    @pl.when(b == 0)
    def _():
        lon = lon_ref[...]
        out_ref[16] = (lon >> 3).astype(jnp.float32).astype(jnp.bfloat16)
        out_ref[17] = ((lon & 7) * LEVELS + level_ref[...]).astype(jnp.float32).astype(jnp.bfloat16)

    members, nobs = out_ref.shape[1], out_ref.shape[2]
    lons = ens_ref.shape[2]
    step = 256
    lon = lon_ref[pl.ds(b, 1), :]
    level = level_ref[pl.ds(b, 1), :]
    place = lax.broadcasted_iota(jnp.int32, (step, nobs), 0).astype(jnp.float32)
    place = place.astype(jnp.bfloat16)
    onehot = []
    for s in range(0, lons, step):
        away = jnp.broadcast_to((lon - s).astype(jnp.float32), (16, nobs)).astype(jnp.bfloat16)
        away = jnp.concatenate([away] * (step // 16), axis=0)
        onehot.append(jnp.where(place == away, jnp.bfloat16(1), jnp.bfloat16(0)))
    total = jnp.dot(
        ens_ref[0], jnp.concatenate(onehot, axis=0), preferred_element_type=jnp.float32
    )
    mine = lax.broadcasted_iota(jnp.int32, (LEVELS, nobs), 0) == level
    total = jnp.where(mine[None], total.reshape(members, LEVELS, nobs), 0.0)
    out_ref[b] = jnp.sum(total, axis=1).astype(jnp.bfloat16)


def pick(obs_level, obs_lon, ensemble):
    rows, width, lons = ensemble.shape
    nobs = obs_lon.shape[1]
    whole = pl.BlockSpec((rows, nobs), lambda b: (0, 0))
    return pl.pallas_call(
        pick_kernel,
        grid=(rows,),
        in_specs=[whole, whole, pl.BlockSpec((1, width, lons), lambda b: (b, 0, 0))],
        out_specs=pl.BlockSpec((PLANES, rows, nobs), lambda b: (0, 0, 0)),
        out_shape=jax.ShapeDtypeStruct((PLANES, rows, nobs), jnp.bfloat16),
        compiler_params=params(),
        name="pick",
    )(obs_level, obs_lon, ensemble)


def column(loc_ref, m):
    row = loc_ref[pl.ds(m, 1), :]
    return jnp.broadcast_to(row, (128, row.shape[1])).T


def legendre_kernel(leg_ref, control_ref, loc_ref, out_ref, acc_ref):
    m = pl.program_id(0)
    slots = pl.num_programs(0)
    lats = out_ref.shape[0]
    width = control_ref.shape[3]
    loc = column(loc_ref, m)
    scaled = [
        (control_ref[0, c].astype(jnp.float32) * loc).astype(jnp.bfloat16) for c in range(2)
    ]
    got = lax.dot_general(
        leg_ref[0],
        jnp.concatenate(scaled, axis=1),
        (((0,), (0,)), ((), ())),
        preferred_element_type=jnp.float32,
    )
    for c in range(2):
        acc_ref[pl.ds(c * ROWS + m, lats, stride=PITCH), :] = got[:, c * width : (c + 1) * width]

    @pl.when(m == slots - 1)
    def _():
        def move(i, carry):
            for k in range(16):
                b = i * 16 + k
                out_ref[b] = acc_ref[pl.ds(b * PITCH, 2 * ROWS), :].astype(jnp.bfloat16)
            return carry

        lax.fori_loop(0, lats // 16, move, 0)


def legendre_forward(legendre, control, loc):
    slots, _, degs, width = control.shape
    lats = legendre.shape[2]
    return pl.pallas_call(
        legendre_kernel,
        grid=(slots,),
        in_specs=[
            pl.BlockSpec((1, degs, lats), lambda m: (m, 0, 0)),
            pl.BlockSpec((1, 2, degs, width), lambda m: (m, 0, 0, 0)),
            pl.BlockSpec((slots, degs), lambda m: (0, 0)),
        ],
        out_specs=pl.BlockSpec((lats, 2 * slots, width), lambda m: (0, 0, 0)),
        out_shape=jax.ShapeDtypeStruct((lats, 2 * slots, width), jnp.bfloat16),
        scratch_shapes=[pltpu.VMEM((lats * PITCH, width), jnp.float32)],
        compiler_params=params(),
        cost_estimate=pl.CostEstimate(
            flops=2 * slots * degs * lats * 2 * width, bytes_accessed=16 * 2**20, transcendentals=0
        ),
        name="legendre_forward",
    )(legendre, control, loc)


def forward_kernel(ids_ref, e_ref, coeff_ref, order_ref, *rest):
    part_ref, four_ref, keep_ref, lon_ref, lev_ref, ens_ref = rest[-6:]
    hi = e_ref[0, 16].astype(jnp.float32)
    lo = e_ref[0, 17].astype(jnp.float32)
    low = jnp.floor(lo * (1.0 / LEVELS))
    lon_ref[...] = hi * 8.0 + low
    lev_ref[...] = lo - low * LEVELS
    keep_ref[0] = e_ref[0]
    members, nobs = e_ref.shape[2], e_ref.shape[3]
    ens_ref[...] = e_ref[0, :ROWS].astype(jnp.float32)
    order = order_ref[...]
    slots = order.shape[0]
    grid_level = lax.broadcasted_iota(jnp.int32, (LEVELS, nobs), 0).astype(jnp.float32)

    def one(b):
        turns = order * lon_ref[pl.ds(b, 1), :]
        frac = turns - jnp.floor(turns + 0.5)
        square = frac * frac
        sine = frac * horner(HALF_SIN, square)
        cosine = horner(HALF_COS, square)
        four = jnp.concatenate(
            [(1.0 - sine * sine).astype(jnp.bfloat16), (sine * cosine).astype(jnp.bfloat16)],
            axis=0,
        )
        four_ref[0, b] = four
        field = lax.dot_general(
            coeff_ref[b], four, (((0,), (0,)), ((), ())), preferred_element_type=jnp.float32
        )
        total = None
        for k in range(members):
            ens = ens_ref[b, k : k + 1]
            term = field[k * LEVELS : (k + 1) * LEVELS] * ens
            total = term if total is None else total + term
        mine = grid_level == lev_ref[pl.ds(b, 1), :]
        part_ref[pl.ds(b, 1), :] = jnp.sum(jnp.where(mine, total, 0.0), axis=0, keepdims=True)

    for b in range(ROWS):
        one(b)


def forward(ids, e, coeff, order, before):
    n = e.shape[0]
    lats, modes, width = coeff.shape
    nobs = e.shape[3]
    blocks = lats // ROWS
    whole = pl.BlockSpec(order.shape, lambda i, ids: (0, 0))
    e_spec = lambda f: pl.BlockSpec((1, PLANES, ROWS, nobs), f)
    at_ids = lambda i, ids: (ids[i], 0, 0, 0)
    out_shape = (
        jax.ShapeDtypeStruct((lats, nobs), jnp.float32),
        jax.ShapeDtypeStruct((blocks, ROWS, modes, nobs), jnp.bfloat16),
        jax.ShapeDtypeStruct((blocks, PLANES, ROWS, nobs), jnp.bfloat16),
    )
    passed = () if before is None else tuple(before)
    return pl.pallas_call(
        forward_kernel,
        grid_spec=pltpu.PrefetchScalarGridSpec(
            num_scalar_prefetch=1,
            grid=(n,),
            in_specs=[
                e_spec(lambda i, ids: (i, 0, 0, 0)),
                pl.BlockSpec((ROWS, modes, width), lambda i, ids: (ids[i], 0, 0)),
                whole,
            ]
            + [pl.BlockSpec(memory_space=pl.ANY)] * len(passed),
            out_specs=(
                pl.BlockSpec((ROWS, nobs), lambda i, ids: (ids[i], 0)),
                pl.BlockSpec((1, ROWS, modes, nobs), at_ids),
                e_spec(at_ids),
            ),
            scratch_shapes=[
                pltpu.VMEM((ROWS, nobs), jnp.float32),
                pltpu.VMEM((ROWS, nobs), jnp.float32),
                pltpu.VMEM((ROWS, ROWS, nobs), jnp.float32),
            ],
        ),
        out_shape=out_shape,
        input_output_aliases={4 + i: i for i in range(len(passed))},
        compiler_params=params(),
        cost_estimate=pl.CostEstimate(
            flops=n * 2 * 10**9, bytes_accessed=n * 2**20, transcendentals=0
        ),
        name="observe",
    )(ids, e, coeff, order, *passed)


def backward_kernel(
    e_ref, four_ref, misfit_ref, leg_ref, control_ref, weighted_ref, out_ref,
    back_ref, lev_ref, ens_ref,
):
    step = pl.program_id(0)
    blocks = misfit_ref.shape[0] // ROWS
    nobs = misfit_ref.shape[1]
    members = e_ref.shape[2]
    modes = four_ref.shape[2]
    lats = misfit_ref.shape[0]
    width = control_ref.shape[3]

    @pl.when(step < blocks)
    def _():
        lo = e_ref[0, 17].astype(jnp.float32)
        lev_ref[...] = lo - jnp.floor(lo * (1.0 / LEVELS)) * LEVELS
        grid_level = lax.broadcasted_iota(jnp.int32, (LEVELS, nobs), 0).astype(jnp.float32)
        for b in range(ROWS):
            misfit = misfit_ref[pl.ds(step * ROWS + b, 1), :]
            ens_ref[b] = e_ref[0, b].astype(jnp.float32) * misfit

        def one(b):
            mine = grid_level == lev_ref[pl.ds(b, 1), :]
            spread = [
                jnp.where(mine, ens_ref[b, k : k + 1], 0.0)
                for k in range(members)
            ]
            back_ref[pl.ds((step * ROWS + b) * PITCH, modes), :] = lax.dot_general(
                four_ref[0, b],
                jnp.concatenate(spread, axis=0).astype(jnp.bfloat16),
                (((1,), (1,)), ((), ())),
                preferred_element_type=jnp.float32,
            )

        for b in range(ROWS):
            one(b)

    @pl.when(step >= blocks)
    def _():
        m = step - blocks
        pieces = [
            back_ref[pl.ds(c * ROWS + m, lats, stride=PITCH), :].astype(jnp.bfloat16)
            for c in range(2)
        ]
        got = jnp.dot(
            leg_ref[0], jnp.concatenate(pieces, axis=1), preferred_element_type=jnp.float32
        )
        loc = column(weighted_ref, m)
        for c in range(2):
            out_ref[0, c] = (
                control_ref[0, c].astype(jnp.float32) + loc * got[:, c * width : (c + 1) * width]
            )


def backward(e, four, misfit, legendre, control, loc):
    blocks, _, _, nobs = e.shape
    modes = four.shape[2]
    slots, _, degs, width = control.shape
    lats = legendre.shape[2]
    first = lambda s: jnp.minimum(s, blocks - 1)
    second = lambda s: jnp.maximum(s - blocks, 0)
    per_slot = pl.BlockSpec((1, 2, degs, width), lambda s: (second(s), 0, 0, 0))
    return pl.pallas_call(
        backward_kernel,
        grid=(blocks + slots,),
        in_specs=[
            pl.BlockSpec((1, PLANES, ROWS, nobs), lambda s: (first(s), 0, 0, 0)),
            pl.BlockSpec((1, ROWS, modes, nobs), lambda s: (first(s), 0, 0, 0)),
            pl.BlockSpec((lats, nobs), lambda s: (0, 0)),
            pl.BlockSpec((1, degs, lats), lambda s: (second(s), 0, 0)),
            per_slot,
            pl.BlockSpec((slots, degs), lambda s: (0, 0)),
        ],
        out_specs=per_slot,
        out_shape=jax.ShapeDtypeStruct(control.shape, jnp.float32),
        scratch_shapes=[
            pltpu.VMEM((lats * PITCH, width), jnp.float32),
            pltpu.VMEM((ROWS, nobs), jnp.float32),
            pltpu.VMEM((ROWS, ROWS, nobs), jnp.float32),
        ],
        compiler_params=params(),
        name="adjoint",
    )(e, four, misfit, legendre, control, loc)


def shift(x, dz=0, dy=0, dx=0):
    pairs = []
    for w in range(32):
        z, y, h = w // 8, w // 2 % 4, w % 2
        pairs.append((w, (z + dz) % 4 * 8 + (y + dy) % 4 * 2 + (h + dx) % 2))
    return lax.ppermute(x, "wide", pairs)


def body(
    control, legendre, loc_spectrum, ensemble, order_map, obs_level, obs_lon, obs_value, obs_weight
):
    slots, _, _, width = control.shape
    nobs = obs_lon.shape[1]
    both = ("wide", "narrow")
    w = lax.axis_index("wide")
    n = lax.axis_index("narrow")
    z, y, h = w // 8, w // 2 % 4, w % 2

    def place(dz, dy, dx=0):
        return (z + dz) % 4 * 8 + (y + dy) % 4 * 2 + (h + dx) % 2

    order = lax.dynamic_slice(order_map, (w * slots,), (slots,))
    weighted = jnp.where(order == 0, 1.0, 2.0).astype(jnp.float32)[:, None] * loc_spectrum
    order = order.astype(jnp.float32)[:, None] * (1.0 / ensemble.shape[2])
    order = jnp.broadcast_to(order, (slots, nobs))

    own = pick(obs_level, obs_lon, ensemble)

    half = PLANES // 2

    def ring4(x, cut, **axis):
        (name, _), = axis.items()
        one = shift(x, **{name: 1})
        three = shift(x, **{name: -1})
        two = (shift(one[:cut], **{name: 1}), shift(three[cut:], **{name: -1}))
        return one, two, three

    other = shift(own, dx=1)
    a1, a2, a3 = ring4(own, half, dy=1)
    a = jnp.concatenate([own, a1, *a2, a3], axis=0)
    x1, x2, x3 = ring4(other, half, dz=1)
    x = jnp.concatenate([other, x1, *x2, x3], axis=0)
    az1, az2, az3 = ring4(a, 2 * PLANES, dz=1)
    xy1, xy2, xy3 = ring4(x, 2 * PLANES, dy=1)

    steps = (0, -1, -2, 1)
    a_ids = lambda dz: [place(dz, s) for s in steps]
    x_ids = lambda dy: [place(s, dy, 1) for s in steps]
    far = lambda t: jnp.concatenate(t, axis=0)
    chunks = [
        (a, a_ids(0)),
        (x, x_ids(0)),
        (az1, a_ids(-1)),
        (az3, a_ids(1)),
        (xy1, x_ids(-1)),
        (xy3, x_ids(1)),
        (far(az2), a_ids(-2)),
        (far(xy2), x_ids(-2)),
    ]
    coeff = legendre_forward(legendre, control, weighted)
    state = None
    for e, ids in chunks:
        e = e.reshape(-1, PLANES, ROWS, nobs)
        state = forward(jnp.stack(ids).astype(jnp.int32), e, coeff, order, state)
    part, four, e_all = state

    devices = lax.axis_size(both)
    mine = part.shape[0] // devices
    parts = lax.all_to_all(part, both, split_axis=0, concat_axis=0, tiled=True)
    picked = jnp.sum(parts.reshape(devices, mine, nobs), axis=0)
    value = lax.dynamic_slice_in_dim(obs_value, n * mine, mine, 0)
    weight = lax.dynamic_slice_in_dim(obs_weight, n * mine, mine, 0)
    misfit = weight * (picked - value)
    misfit = jnp.broadcast_to(misfit[None], (devices, mine, nobs)).reshape(part.shape)
    misfit = lax.all_to_all(misfit, both, split_axis=0, concat_axis=0, tiled=True)
    return backward(e_all, four, misfit, legendre, control, weighted)


def solution(mesh):
    rows = P("wide", None)
    return jax.shard_map(
        body,
        mesh=mesh,
        in_specs=(
            P("wide", None, None, "narrow"),
            P("wide", None, None),
            rows,
            P("wide", "narrow", None),
            P(),
            rows,
            rows,
            rows,
            rows,
        ),
        out_specs=P("wide", None, None, "narrow"),
        check_vma=False,
    )
```

```python
import jax
import jax.numpy as jnp
from jax import lax
from jax.experimental import pallas as pl
from jax.experimental.pallas import tpu as pltpu
from jax.sharding import PartitionSpec as P

LEVELS = 8
ROWS = 16
PLANES = 18
PICK = 4
ORDERS = 2
BLOCKS = 2
PITCH = 33
SIN = (6.2831851595779975, -41.34165492085311, 81.60099762205961, -76.54964290998956, 39.53570242643394)
COS = (0.9999999532360554, -19.739171315085017, 64.93458093602055, -85.24007915837501, 56.24034662339592)
HALF_SIN = tuple(2**0.5 * c / 2 ** (2 * i + 1) for i, c in enumerate(SIN))
HALF_COS = tuple(-(2**0.5) * c / 4**i for i, c in enumerate(COS))


def params(mib):
    return pltpu.CompilerParams(vmem_limit_bytes=mib * 2**20)


def in_hbm(x):
    return pltpu.with_memory_space_constraint(x, pltpu.HBM)


def horner(coefs, x):
    total = jnp.full_like(x, coefs[-1])
    for c in coefs[-2::-1]:
        total = total * x + c
    return total


def pick_kernel(level_ref, lon_ref, ens_ref, out_ref):
    b0 = pl.program_id(0) * PICK

    @pl.when(b0 == 0)
    def _():
        lon = lon_ref[...]
        out_ref[16] = (lon >> 3).astype(jnp.float32).astype(jnp.bfloat16)
        out_ref[17] = ((lon & 7) * LEVELS + level_ref[...]).astype(jnp.float32).astype(jnp.bfloat16)

    members, nobs = out_ref.shape[1], out_ref.shape[2]
    lons = ens_ref.shape[2]
    step = 256
    place = lax.broadcasted_iota(jnp.int32, (step, nobs), 0).astype(jnp.float32)
    place = place.astype(jnp.bfloat16)
    for k in range(PICK):
        lon = lon_ref[pl.ds(b0 + k, 1), :]
        level = level_ref[pl.ds(b0 + k, 1), :]
        onehot = []
        for s in range(0, lons, step):
            away = jnp.broadcast_to((lon - s).astype(jnp.float32), (16, nobs)).astype(jnp.bfloat16)
            away = jnp.concatenate([away] * (step // 16), axis=0)
            onehot.append(jnp.where(place == away, jnp.bfloat16(1), jnp.bfloat16(0)))
        total = jnp.dot(
            ens_ref[k], jnp.concatenate(onehot, axis=0), preferred_element_type=jnp.float32
        )
        mine = lax.broadcasted_iota(jnp.int32, (LEVELS, nobs), 0) == level
        total = jnp.where(mine[None], total.reshape(members, LEVELS, nobs), 0.0)
        out_ref[b0 + k] = jnp.sum(total, axis=1).astype(jnp.bfloat16)


def pick(obs_level, obs_lon, ensemble):
    rows, width, lons = ensemble.shape
    nobs = obs_lon.shape[1]
    whole = pl.BlockSpec((rows, nobs), lambda b: (0, 0))
    return pl.pallas_call(
        pick_kernel,
        grid=(rows // PICK,),
        in_specs=[whole, whole, pl.BlockSpec((PICK, width, lons), lambda b: (b, 0, 0))],
        out_specs=pl.BlockSpec((PLANES, rows, nobs), lambda b: (0, 0, 0)),
        out_shape=jax.ShapeDtypeStruct((PLANES, rows, nobs), jnp.bfloat16),
        compiler_params=params(12),
        name="pick",
    )(obs_level, obs_lon, in_hbm(ensemble))


def column(loc_ref, m):
    row = loc_ref[pl.ds(m, 1), :]
    return jnp.broadcast_to(row, (128, row.shape[1])).T


def legendre_kernel(leg_ref, control_ref, loc_ref, out_ref, acc_ref):
    step = pl.program_id(0)
    lats = out_ref.shape[0]
    width = control_ref.shape[3]
    for k in range(ORDERS):
        m = step * ORDERS + k
        loc = column(loc_ref, m)
        scaled = [
            (control_ref[k, c].astype(jnp.float32) * loc).astype(jnp.bfloat16) for c in range(2)
        ]
        got = lax.dot_general(
            leg_ref[k],
            jnp.concatenate(scaled, axis=1),
            (((0,), (0,)), ((), ())),
            preferred_element_type=jnp.float32,
        )
        for c in range(2):
            acc_ref[pl.ds(c * ROWS + m, lats, stride=PITCH), :] = got[
                :, c * width : (c + 1) * width
            ]

    @pl.when(step == pl.num_programs(0) - 1)
    def _():
        def move(i, carry):
            for k in range(16):
                b = i * 16 + k
                out_ref[b] = acc_ref[pl.ds(b * PITCH, 2 * ROWS), :].astype(jnp.bfloat16)
            return carry

        lax.fori_loop(0, lats // 16, move, 0)


def legendre_forward(legendre, control, loc):
    slots, _, degs, width = control.shape
    lats = legendre.shape[2]
    return pl.pallas_call(
        legendre_kernel,
        grid=(slots // ORDERS,),
        in_specs=[
            pl.BlockSpec((ORDERS, degs, lats), lambda m: (m, 0, 0)),
            pl.BlockSpec((ORDERS, 2, degs, width), lambda m: (m, 0, 0, 0)),
            pl.BlockSpec((slots, degs), lambda m: (0, 0)),
        ],
        out_specs=pl.BlockSpec((lats, 2 * slots, width), lambda m: (0, 0, 0)),
        out_shape=jax.ShapeDtypeStruct((lats, 2 * slots, width), jnp.bfloat16),
        scratch_shapes=[pltpu.VMEM((lats * PITCH, width), jnp.float32)],
        compiler_params=params(22),
        cost_estimate=pl.CostEstimate(
            flops=2 * slots * degs * lats * 2 * width, bytes_accessed=16 * 2**20, transcendentals=0
        ),
        name="legendre_forward",
    )(in_hbm(legendre), in_hbm(control), loc)


def forward_kernel(place_ref, e_ref, coeff_ref, order_ref, *rest):
    part_ref, four_ref, keep_ref, lon_ref, lev_ref, ens_ref, sum_ref = rest[-7:]
    hi = e_ref[0, 16].astype(jnp.float32)
    lo = e_ref[0, 17].astype(jnp.float32)
    low = jnp.floor(lo * (1.0 / LEVELS))
    lon_ref[...] = hi * 8.0 + low
    lev_ref[...] = lo - low * LEVELS
    keep_ref[0] = e_ref[0]
    members, nobs = e_ref.shape[2], e_ref.shape[3]
    ens_ref[...] = e_ref[0, :ROWS].astype(jnp.float32)
    order = order_ref[...]
    slots = order.shape[0]
    grid_level = lax.broadcasted_iota(jnp.int32, (LEVELS, nobs), 0).astype(jnp.float32)

    def one(b):
        turns = order * lon_ref[pl.ds(b, 1), :]
        frac = turns - jnp.floor(turns + 0.5)
        square = frac * frac
        sine = frac * horner(HALF_SIN, square)
        cosine = horner(HALF_COS, square)
        four = jnp.concatenate(
            [(1.0 - sine * sine).astype(jnp.bfloat16), (sine * cosine).astype(jnp.bfloat16)],
            axis=0,
        )
        four_ref[0, b] = four
        field = lax.dot_general(
            coeff_ref[b], four, (((0,), (0,)), ((), ())), preferred_element_type=jnp.float32
        )
        total = None
        for k in range(members):
            ens = ens_ref[b, k : k + 1]
            term = field[k * LEVELS : (k + 1) * LEVELS] * ens
            total = term if total is None else total + term
        mine = grid_level == lev_ref[pl.ds(b, 1), :]
        total = jnp.sum(jnp.where(mine, total, 0.0), axis=0, keepdims=True)
        for lane in range(0, nobs, 128):
            sum_ref[pl.ds((b * nobs + lane) // 128, 1), :] = total[:, lane : lane + 128]

    for b in range(ROWS):
        one(b)
    part_ref[...] = sum_ref[...].astype(jnp.bfloat16)


def forward(where, along, offset, e, coeff, order, before):
    n = e.shape[0]
    lats, modes, width = coeff.shape
    nobs = e.shape[3]
    blocks = lats // ROWS
    lanes = nobs // 128

    def block(i, place):
        z, y, h = (place[d] + offset[d] for d in range(3))
        z, y = (z - i, y) if along == "z" else (z, y - i)
        return (z & 3) * 8 + (y & 3) * 2 + (h & 1)

    e_spec = lambda f: pl.BlockSpec((1, PLANES, ROWS, nobs), f)
    at_block = lambda i, place: (block(i, place), 0, 0, 0)
    out_shape = (
        jax.ShapeDtypeStruct((lats * lanes, 128), jnp.bfloat16),
        jax.ShapeDtypeStruct((blocks, ROWS, modes, nobs), jnp.bfloat16),
        jax.ShapeDtypeStruct((blocks, PLANES, ROWS, nobs), jnp.bfloat16),
    )
    passed = () if before is None else tuple(before)
    return pl.pallas_call(
        forward_kernel,
        grid_spec=pltpu.PrefetchScalarGridSpec(
            num_scalar_prefetch=1,
            grid=(n,),
            in_specs=[
                e_spec(lambda i, place: (i, 0, 0, 0)),
                pl.BlockSpec((ROWS, modes, width), lambda i, place: (block(i, place), 0, 0)),
                pl.BlockSpec(order.shape, lambda i, place: (0, 0)),
            ]
            + [pl.BlockSpec(memory_space=pl.ANY)] * len(passed),
            out_specs=(
                pl.BlockSpec((ROWS * lanes, 128), lambda i, place: (block(i, place), 0)),
                pl.BlockSpec((1, ROWS, modes, nobs), at_block),
                e_spec(at_block),
            ),
            scratch_shapes=[
                pltpu.VMEM((ROWS, nobs), jnp.float32),
                pltpu.VMEM((ROWS, nobs), jnp.float32),
                pltpu.VMEM((ROWS, ROWS, nobs), jnp.float32),
                pltpu.VMEM((ROWS * lanes, 128), jnp.float32),
            ],
        ),
        out_shape=out_shape,
        input_output_aliases={4 + i: i for i in range(len(passed))},
        compiler_params=params(6),
        cost_estimate=pl.CostEstimate(
            flops=n * 6 * 10**8, bytes_accessed=n * 2**19, transcendentals=0
        ),
        name="observe",
    )(where, e, coeff, order, *passed)


def backward_kernel(
    e_ref, four_ref, misfit_ref, leg_ref, control_ref, weighted_ref, out_ref,
    back_ref, lev_ref, ens_ref, misfit32_ref,
):
    step = pl.program_id(0)
    nobs = e_ref.shape[3]
    members = e_ref.shape[2]
    modes = four_ref.shape[2]
    lats = back_ref.shape[0] // PITCH
    width = control_ref.shape[3]
    steps = lats // (ROWS * BLOCKS)

    @pl.when(step < steps)
    def _():
        misfit32_ref[...] = misfit_ref[...].astype(jnp.float32)
        grid_level = lax.broadcasted_iota(jnp.int32, (LEVELS, nobs), 0).astype(jnp.float32)
        for g in range(BLOCKS):
            lo = e_ref[g, 17].astype(jnp.float32)
            lev_ref[g] = lo - jnp.floor(lo * (1.0 / LEVELS)) * LEVELS
            for b in range(ROWS):
                row = (g * ROWS + b) * nobs // 128
                misfit = jnp.concatenate(
                    [
                        jnp.broadcast_to(misfit32_ref[row + lane : row + lane + 1], (members, 128))
                        for lane in range(nobs // 128)
                    ],
                    axis=1,
                )
                ens_ref[g, b] = e_ref[g, b].astype(jnp.float32) * misfit
            for b in range(ROWS):
                mine = grid_level == lev_ref[g, b : b + 1]
                spread = [
                    jnp.where(mine, ens_ref[g, b, k : k + 1], 0.0) for k in range(members)
                ]
                lat = (step * BLOCKS + g) * ROWS + b
                back_ref[pl.ds(lat * PITCH, modes), :] = lax.dot_general(
                    four_ref[g, b],
                    jnp.concatenate(spread, axis=0).astype(jnp.bfloat16),
                    (((1,), (1,)), ((), ())),
                    preferred_element_type=jnp.float32,
                )

    @pl.when(step >= steps)
    def _():
        for k in range(ORDERS):
            m = (step - steps) * ORDERS + k
            pieces = [
                back_ref[pl.ds(c * ROWS + m, lats, stride=PITCH), :].astype(jnp.bfloat16)
                for c in range(2)
            ]
            got = jnp.dot(
                leg_ref[k], jnp.concatenate(pieces, axis=1), preferred_element_type=jnp.float32
            )
            loc = column(weighted_ref, m)
            for c in range(2):
                out_ref[k, c] = (
                    control_ref[k, c].astype(jnp.float32)
                    + loc * got[:, c * width : (c + 1) * width]
                )


def backward(e, four, misfit, legendre, control, loc):
    blocks, _, _, nobs = e.shape
    modes = four.shape[2]
    slots, _, degs, width = control.shape
    lats = legendre.shape[2]
    lanes = nobs // 128
    steps = blocks // BLOCKS
    first = lambda s: jnp.minimum(s, steps - 1)
    second = lambda s: jnp.maximum(s - steps, 0)
    per_slot = pl.BlockSpec((ORDERS, 2, degs, width), lambda s: (second(s), 0, 0, 0))
    return pl.pallas_call(
        backward_kernel,
        grid=(steps + slots // ORDERS,),
        in_specs=[
            pl.BlockSpec((BLOCKS, PLANES, ROWS, nobs), lambda s: (first(s), 0, 0, 0)),
            pl.BlockSpec((BLOCKS, ROWS, modes, nobs), lambda s: (first(s), 0, 0, 0)),
            pl.BlockSpec((BLOCKS * ROWS * lanes, 128), lambda s: (first(s), 0)),
            pl.BlockSpec((ORDERS, degs, lats), lambda s: (second(s), 0, 0)),
            per_slot,
            pl.BlockSpec((slots, degs), lambda s: (0, 0)),
        ],
        out_specs=per_slot,
        out_shape=jax.ShapeDtypeStruct(control.shape, jnp.float32),
        scratch_shapes=[
            pltpu.VMEM((lats * PITCH, width), jnp.float32),
            pltpu.VMEM((BLOCKS, ROWS, nobs), jnp.float32),
            pltpu.VMEM((BLOCKS, ROWS, ROWS, nobs), jnp.float32),
            pltpu.VMEM((BLOCKS * ROWS * lanes, 128), jnp.float32),
        ],
        compiler_params=params(24),
        name="adjoint",
    )(e, four, misfit, in_hbm(legendre), in_hbm(control), loc)


def shift(x, dz=0, dy=0, dx=0):
    pairs = []
    for w in range(32):
        z, y, h = w // 8, w // 2 % 4, w % 2
        pairs.append((w, (z + dz) % 4 * 8 + (y + dy) % 4 * 2 + (h + dx) % 2))
    return lax.ppermute(x, "wide", pairs)


def body(
    control, legendre, loc_spectrum, ensemble, order_map, obs_level, obs_lon, obs_value, obs_weight
):
    slots, _, _, width = control.shape
    nobs = obs_lon.shape[1]
    both = ("wide", "narrow")
    w = lax.axis_index("wide")
    n = lax.axis_index("narrow")
    z, y, h = w // 8, w // 2 % 4, w % 2

    order = lax.dynamic_slice(order_map, (w * slots,), (slots,))
    weighted = jnp.where(order == 0, 1.0, 2.0).astype(jnp.float32)[:, None] * loc_spectrum
    order = order.astype(jnp.float32)[:, None] * (1.0 / ensemble.shape[2])
    order = jnp.broadcast_to(order, (slots, nobs))

    own = pick(obs_level, obs_lon, ensemble)

    def ring4(x, axis):
        return tuple(shift(x, **{axis: k}) for k in (1, 2, 3))

    other = shift(own, dx=1)
    a = jnp.concatenate([own, *ring4(own, "dy")], axis=0)
    x = jnp.concatenate([other, *ring4(other, "dz")], axis=0)
    az = ring4(a, "dz")
    xy = ring4(x, "dy")

    coeff = legendre_forward(legendre, control, weighted)
    where = jnp.stack([z, y, h]).astype(jnp.int32)
    state = None
    chunks = [("y", (0, 0, 0), a), ("z", (0, 0, 1), x)]
    for k in (0, 2, 1):
        chunks += [("y", (-1 - k, 0, 0), az[k]), ("z", (0, -1 - k, 1), xy[k])]
    for along, offset, e in chunks:
        e = e.reshape(-1, PLANES, ROWS, nobs)
        state = forward(where, along, offset, e, coeff, order, state)
    part, four, e_all = state

    devices = lax.axis_size(both)
    mine = obs_lon.shape[0] * lax.axis_size("wide") // devices
    tile = mine * nobs // 128
    parts = lax.all_to_all(
        part.reshape(devices, tile, 128), both, split_axis=0, concat_axis=0, tiled=True
    )
    picked = jnp.sum(parts.astype(jnp.float32), axis=0)
    value = lax.dynamic_slice_in_dim(obs_value, n * mine, mine, 0).reshape(tile, 128)
    weight = lax.dynamic_slice_in_dim(obs_weight, n * mine, mine, 0).reshape(tile, 128)
    misfit = (weight * (picked - value)).astype(jnp.bfloat16)
    misfit = jnp.broadcast_to(misfit[None], (devices, tile, 128))
    misfit = lax.all_to_all(misfit, both, split_axis=0, concat_axis=0, tiled=True)
    return backward(e_all, four, misfit.reshape(part.shape), legendre, control, weighted)


def solution(mesh):
    rows = P("wide", None)
    return jax.shard_map(
        body,
        mesh=mesh,
        in_specs=(
            P("wide", None, None, "narrow"),
            P("wide", None, None),
            rows,
            P("wide", "narrow", None),
            P(),
            rows,
            rows,
            rows,
            rows,
        ),
        out_specs=P("wide", None, None, "narrow"),
        check_vma=False,
    )
```

```python
import jax
import jax.numpy as jnp
from jax import lax
from jax.experimental import pallas as pl
from jax.experimental.pallas import tpu as pltpu
from jax.sharding import PartitionSpec as P


LEVELS = 8
ROWS = 16
PLANES = 18
PICK = 4
ORDERS = 2
BLOCKS = 2
PITCH = 33
SIN = (6.2831851595779975, -41.34165492085311, 81.60099762205961, -76.54964290998956, 39.53570242643394)
COS = (0.9999999532360554, -19.739171315085017, 64.93458093602055, -85.24007915837501, 56.24034662339592)
HALF_SIN = tuple(2**0.5 * c / 2 ** (2 * i + 1) for i, c in enumerate(SIN))
HALF_COS = tuple(-(2**0.5) * c / 4**i for i, c in enumerate(COS))


def params(mib):
    return pltpu.CompilerParams(vmem_limit_bytes=mib * 2**20)


def in_hbm(x):
    return pltpu.with_memory_space_constraint(x, pltpu.HBM)


def horner(coefs, x):
    total = jnp.full_like(x, coefs[-1])
    for c in coefs[-2::-1]:
        total = total * x + c
    return total


def pick_kernel(level_ref, lon_ref, ens_ref, out_ref):
    b0 = pl.program_id(0) * PICK

    @pl.when(b0 == 0)
    def _():
        lon = lon_ref[...]
        out_ref[16] = (lon >> 3).astype(jnp.float32).astype(jnp.bfloat16)
        out_ref[17] = ((lon & 7) * LEVELS + level_ref[...]).astype(jnp.float32).astype(jnp.bfloat16)

    members, nobs = out_ref.shape[1], out_ref.shape[2]
    lons = ens_ref.shape[2]
    step = 256
    place = lax.broadcasted_iota(jnp.int32, (step, nobs), 0).astype(jnp.float32)
    place = place.astype(jnp.bfloat16)
    shape = (members, ens_ref.shape[1])
    same = lax.broadcasted_iota(jnp.int32, shape, 1) // LEVELS
    same = (same == lax.broadcasted_iota(jnp.int32, shape, 0)).astype(jnp.float32)
    same = same.astype(jnp.bfloat16)
    for k in range(PICK):
        lon = lon_ref[pl.ds(b0 + k, 1), :]
        level = level_ref[pl.ds(b0 + k, 1), :]
        onehot = []
        for s in range(0, lons, step):
            away = jnp.broadcast_to((lon - s).astype(jnp.float32), (16, nobs)).astype(jnp.bfloat16)
            away = jnp.concatenate([away] * (step // 16), axis=0)
            onehot.append(jnp.where(place == away, jnp.bfloat16(1), jnp.bfloat16(0)))
        total = jnp.dot(
            ens_ref[k], jnp.concatenate(onehot, axis=0), preferred_element_type=jnp.float32
        )
        mine = lax.broadcasted_iota(jnp.int32, (LEVELS, nobs), 0) == level
        total = jnp.where(mine[None], total.reshape(members, LEVELS, nobs), 0.0)
        total = total.reshape(members * LEVELS, nobs).astype(jnp.bfloat16)
        out_ref[b0 + k] = jnp.dot(same, total, preferred_element_type=jnp.float32).astype(
            jnp.bfloat16
        )


def pick(obs_level, obs_lon, ensemble):
    rows, width, lons = ensemble.shape
    nobs = obs_lon.shape[1]
    whole = pl.BlockSpec((rows, nobs), lambda b: (0, 0))
    return pl.pallas_call(
        pick_kernel,
        grid=(rows // PICK,),
        in_specs=[whole, whole, pl.BlockSpec((PICK, width, lons), lambda b: (b, 0, 0))],
        out_specs=pl.BlockSpec((PLANES, rows, nobs), lambda b: (0, 0, 0)),
        out_shape=jax.ShapeDtypeStruct((PLANES, rows, nobs), jnp.bfloat16),
        compiler_params=params(12),
        name="pick",
    )(in_hbm(obs_level), in_hbm(obs_lon), in_hbm(ensemble))


def order_of(order_ref, place_ref, m):
    return order_ref[((place_ref[0] * 4 + place_ref[1]) * 2 + place_ref[2]) * ROWS + m]


def column(loc_ref, m, order):
    row = loc_ref[pl.ds(m, 1), :]
    row = jnp.where(order == 0, row, row * 2.0)
    return jnp.broadcast_to(row, (128, row.shape[1])).T


def legendre_kernel(order_ref, place_ref, leg_ref, control_ref, loc_ref, out_ref, acc_ref):
    step = pl.program_id(0)
    lats = out_ref.shape[0]
    width = control_ref.shape[3]
    for k in range(ORDERS):
        m = step * ORDERS + k
        loc = column(loc_ref, m, order_of(order_ref, place_ref, m))
        scaled = [
            (control_ref[k, c].astype(jnp.float32) * loc).astype(jnp.bfloat16) for c in range(2)
        ]
        got = lax.dot_general(
            leg_ref[k],
            jnp.concatenate(scaled, axis=1),
            (((0,), (0,)), ((), ())),
            preferred_element_type=jnp.float32,
        )
        for c in range(2):
            acc_ref[pl.ds(c * ROWS + m, lats, stride=PITCH), :] = got[
                :, c * width : (c + 1) * width
            ]

    @pl.when(step == pl.num_programs(0) - 1)
    def _():
        def move(i, carry):
            for k in range(16):
                b = i * 16 + k
                out_ref[b] = acc_ref[pl.ds(b * PITCH, 2 * ROWS), :].astype(jnp.bfloat16)
            return carry

        lax.fori_loop(0, lats // 16, move, 0)


def legendre_forward(order_map, where, legendre, control, loc):
    slots, _, degs, width = control.shape
    lats = legendre.shape[2]
    return pl.pallas_call(
        legendre_kernel,
        grid_spec=pltpu.PrefetchScalarGridSpec(
            num_scalar_prefetch=2,
            grid=(slots // ORDERS,),
            in_specs=[
                pl.BlockSpec((ORDERS, degs, lats), lambda m, *_: (m, 0, 0)),
                pl.BlockSpec((ORDERS, 2, degs, width), lambda m, *_: (m, 0, 0, 0)),
                pl.BlockSpec((slots, degs), lambda m, *_: (0, 0)),
            ],
            out_specs=pl.BlockSpec((lats, 2 * slots, width), lambda m, *_: (0, 0, 0)),
            scratch_shapes=[pltpu.VMEM((lats * PITCH, width), jnp.float32)],
        ),
        out_shape=jax.ShapeDtypeStruct((lats, 2 * slots, width), jnp.bfloat16),
        compiler_params=params(22),
        cost_estimate=pl.CostEstimate(
            flops=2 * slots * degs * lats * 2 * width, bytes_accessed=16 * 2**20, transcendentals=0
        ),
        name="legendre_forward",
    )(order_map, where, in_hbm(legendre), in_hbm(control), in_hbm(loc))


def forward_kernel(order_ref, place_ref, e_ref, coeff_ref, *rest):
    part_ref, four_ref, keep_ref, lon_ref, lev_ref, ens_ref, sum_ref, turn_ref = rest[-8:]
    hi = e_ref[0, 16].astype(jnp.float32)
    lo = e_ref[0, 17].astype(jnp.float32)
    low = jnp.floor(lo * (1.0 / LEVELS))
    lon_ref[...] = hi * 8.0 + low
    lev_ref[...] = lo - low * LEVELS
    keep_ref[0] = e_ref[0]
    members, nobs = e_ref.shape[2], e_ref.shape[3]
    ens_ref[...] = e_ref[0, :ROWS].astype(jnp.float32)

    @pl.when(pl.program_id(0) == 0)
    def _():
        row = lax.broadcasted_iota(jnp.int32, turn_ref.shape, 0)
        order = jnp.zeros(turn_ref.shape, jnp.float32)
        for m in range(ROWS):
            order = jnp.where(
                row == m, order_of(order_ref, place_ref, m).astype(jnp.float32), order
            )
        turn_ref[...] = order * (1.0 / 1024.0)

    turn = turn_ref[...]
    grid_level = lax.broadcasted_iota(jnp.int32, (LEVELS, nobs), 0).astype(jnp.float32)

    def one(b):
        turns = turn * lon_ref[pl.ds(b, 1), :]
        frac = turns - jnp.floor(turns + 0.5)
        square = frac * frac
        sine = frac * horner(HALF_SIN, square)
        cosine = horner(HALF_COS, square)
        four = jnp.concatenate(
            [(1.0 - sine * sine).astype(jnp.bfloat16), (sine * cosine).astype(jnp.bfloat16)],
            axis=0,
        )
        four_ref[0, b] = four
        field = lax.dot_general(
            coeff_ref[b], four, (((0,), (0,)), ((), ())), preferred_element_type=jnp.float32
        )
        total = None
        for k in range(members):
            ens = ens_ref[b, k : k + 1]
            term = field[k * LEVELS : (k + 1) * LEVELS] * ens
            total = term if total is None else total + term
        mine = grid_level == lev_ref[pl.ds(b, 1), :]
        total = jnp.sum(jnp.where(mine, total, 0.0), axis=0, keepdims=True)
        for lane in range(0, nobs, 128):
            sum_ref[pl.ds((b * nobs + lane) // 128, 1), :] = total[:, lane : lane + 128]

    for b in range(ROWS):
        one(b)
    part_ref[...] = sum_ref[...].astype(jnp.bfloat16)


def forward(order_map, where, far, e, coeff, before):
    n = e.shape[0]
    lats, modes, width = coeff.shape
    nobs = e.shape[3]
    blocks = lats // ROWS
    lanes = nobs // 128

    def block(i, place):
        near = i >> 1
        turn = (far - near) * place[3]
        z, y = place[0] - far + turn, place[1] - near - turn
        return (z & 3) * 8 + (y & 3) * 2 + ((place[2] + i) & 1)

    e_spec = lambda f: pl.BlockSpec((1, PLANES, ROWS, nobs), f)
    at_block = lambda i, _, place: (block(i, place), 0, 0, 0)
    out_shape = (
        jax.ShapeDtypeStruct((lats * lanes, 128), jnp.bfloat16),
        jax.ShapeDtypeStruct((blocks, ROWS, modes, nobs), jnp.bfloat16),
        jax.ShapeDtypeStruct((blocks, PLANES, ROWS, nobs), jnp.bfloat16),
    )
    passed = () if before is None else tuple(before)
    return pl.pallas_call(
        forward_kernel,
        grid_spec=pltpu.PrefetchScalarGridSpec(
            num_scalar_prefetch=2,
            grid=(n,),
            in_specs=[
                e_spec(lambda i, _, place: (i, 0, 0, 0)),
                pl.BlockSpec((ROWS, modes, width), lambda i, _, place: (block(i, place), 0, 0)),
            ]
            + [pl.BlockSpec(memory_space=pl.ANY)] * len(passed),
            out_specs=(
                pl.BlockSpec((ROWS * lanes, 128), lambda i, _, place: (block(i, place), 0)),
                pl.BlockSpec((1, ROWS, modes, nobs), at_block),
                e_spec(at_block),
            ),
            scratch_shapes=[
                pltpu.VMEM((ROWS, nobs), jnp.float32),
                pltpu.VMEM((ROWS, nobs), jnp.float32),
                pltpu.VMEM((ROWS, ROWS, nobs), jnp.float32),
                pltpu.VMEM((ROWS * lanes, 128), jnp.float32),
                pltpu.VMEM((ROWS, nobs), jnp.float32),
            ],
        ),
        out_shape=out_shape,
        input_output_aliases={4 + i: i for i in range(len(passed))},
        compiler_params=params(6),
        cost_estimate=pl.CostEstimate(
            flops=n * 6 * 10**8, bytes_accessed=n * 2**19, transcendentals=0
        ),
        name="observe",
    )(order_map, where, e, coeff, *passed)


def backward_kernel(
    order_ref, place_ref, e_ref, four_ref, misfit_ref, leg_ref, control_ref, loc_ref, out_ref,
    back_ref, lev_ref, ens_ref, misfit32_ref,
):
    step = pl.program_id(0)
    nobs = e_ref.shape[3]
    members = e_ref.shape[2]
    modes = four_ref.shape[2]
    lats = back_ref.shape[0] // PITCH
    width = control_ref.shape[3]
    steps = lats // (ROWS * BLOCKS)

    @pl.when(step < steps)
    def _():
        misfit32_ref[...] = misfit_ref[...].astype(jnp.float32)
        grid_level = lax.broadcasted_iota(jnp.int32, (LEVELS, nobs), 0).astype(jnp.float32)
        for g in range(BLOCKS):
            lo = e_ref[g, 17].astype(jnp.float32)
            lev_ref[g] = lo - jnp.floor(lo * (1.0 / LEVELS)) * LEVELS
            for b in range(ROWS):
                row = (g * ROWS + b) * nobs // 128
                misfit = jnp.concatenate(
                    [
                        jnp.broadcast_to(misfit32_ref[row + lane : row + lane + 1], (members, 128))
                        for lane in range(nobs // 128)
                    ],
                    axis=1,
                )
                ens_ref[g, b] = e_ref[g, b].astype(jnp.float32) * misfit
            for b in range(ROWS):
                mine = grid_level == lev_ref[g, b : b + 1]
                spread = [
                    jnp.where(mine, ens_ref[g, b, k : k + 1], 0.0) for k in range(members)
                ]
                lat = (step * BLOCKS + g) * ROWS + b
                back_ref[pl.ds(lat * PITCH, modes), :] = lax.dot_general(
                    four_ref[g, b],
                    jnp.concatenate(spread, axis=0).astype(jnp.bfloat16),
                    (((1,), (1,)), ((), ())),
                    preferred_element_type=jnp.float32,
                )

    @pl.when(step >= steps)
    def _():
        for k in range(ORDERS):
            m = (step - steps) * ORDERS + k
            pieces = [
                back_ref[pl.ds(c * ROWS + m, lats, stride=PITCH), :].astype(jnp.bfloat16)
                for c in range(2)
            ]
            got = jnp.dot(
                leg_ref[k], jnp.concatenate(pieces, axis=1), preferred_element_type=jnp.float32
            )
            loc = column(loc_ref, m, order_of(order_ref, place_ref, m))
            for c in range(2):
                out_ref[k, c] = (
                    control_ref[k, c].astype(jnp.float32)
                    + loc * got[:, c * width : (c + 1) * width]
                )


def backward(order_map, where, e, four, misfit, legendre, control, loc):
    blocks, _, _, nobs = e.shape
    modes = four.shape[2]
    slots, _, degs, width = control.shape
    lats = legendre.shape[2]
    lanes = nobs // 128
    steps = blocks // BLOCKS
    first = lambda s: jnp.minimum(s, steps - 1)
    second = lambda s: jnp.maximum(s - steps, 0)
    per_slot = pl.BlockSpec((ORDERS, 2, degs, width), lambda s, *_: (second(s), 0, 0, 0))
    return pl.pallas_call(
        backward_kernel,
        grid_spec=pltpu.PrefetchScalarGridSpec(
            num_scalar_prefetch=2,
            grid=(steps + slots // ORDERS,),
            in_specs=[
                pl.BlockSpec((BLOCKS, PLANES, ROWS, nobs), lambda s, *_: (first(s), 0, 0, 0)),
                pl.BlockSpec((BLOCKS, ROWS, modes, nobs), lambda s, *_: (first(s), 0, 0, 0)),
                pl.BlockSpec((BLOCKS * ROWS * lanes, 128), lambda s, *_: (first(s), 0)),
                pl.BlockSpec((ORDERS, degs, lats), lambda s, *_: (second(s), 0, 0)),
                per_slot,
                pl.BlockSpec((slots, degs), lambda s, *_: (0, 0)),
            ],
            out_specs=per_slot,
            scratch_shapes=[
                pltpu.VMEM((lats * PITCH, width), jnp.float32),
                pltpu.VMEM((BLOCKS, ROWS, nobs), jnp.float32),
                pltpu.VMEM((BLOCKS, ROWS, ROWS, nobs), jnp.float32),
                pltpu.VMEM((BLOCKS * ROWS * lanes, 128), jnp.float32),
            ],
        ),
        out_shape=jax.ShapeDtypeStruct(control.shape, jnp.float32),
        compiler_params=params(24),
        name="adjoint",
    )(order_map, where, e, four, misfit, in_hbm(legendre), in_hbm(control), in_hbm(loc))


def send(x, distance, stage):
    pairs = []
    for w in range(32):
        for n in range(4):
            z, y, h = w // 8, w // 2 % 4, w % 2
            if stage == "hop":
                h = (h + distance) % 2
            elif (stage == "near") == (n % 2 == 0):
                y = (y + distance) % 4
            else:
                z = (z + distance) % 4
            pairs.append((w * 4 + n, (z * 8 + y * 2 + h) * 4 + n))
    return lax.ppermute(x, ("wide", "narrow"), pairs)


def gather(own):
    pair = jnp.concatenate([own, send(own, 1, "hop")], axis=0)
    near = [pair] + [send(pair, k, "near") for k in (1, 2, 3)]
    near = jnp.concatenate(near, axis=0)
    return [near] + [send(near, k, "far") for k in (1, 2, 3)]


def body(
    control, legendre, loc_spectrum, ensemble, order_map, obs_level, obs_lon, obs_value, obs_weight
):
    nobs = obs_lon.shape[1]
    both = ("wide", "narrow")
    devices = lax.axis_size(both)
    mine = obs_lon.shape[0] * lax.axis_size("wide") // devices
    tile = mine * nobs // 128
    w = lax.axis_index("wide")
    n = lax.axis_index("narrow")
    where = jnp.stack([w >> 3, (w >> 1) & 3, w & 1, n & 1]).astype(jnp.int32)
    own = pick(obs_level, obs_lon, ensemble)

    blocks = gather(own)

    coeff = legendre_forward(order_map, where, legendre, control, loc_spectrum)
    state = None
    for far in (0, 1, 3, 2):
        e = blocks[far].reshape(-1, PLANES, ROWS, nobs)
        state = forward(order_map, where, far, e, coeff, state)
    part, four, e_all = state

    value = lax.dynamic_slice_in_dim(obs_value, n * mine, mine, 0).reshape(tile, 128)
    weight = lax.dynamic_slice_in_dim(obs_weight, n * mine, mine, 0).reshape(tile, 128)
    part, value, weight = lax.optimization_barrier((part, value, weight))
    parts = lax.all_to_all(
        part.reshape(devices, tile, 128), both, split_axis=0, concat_axis=0, tiled=True
    )
    picked = jnp.sum(parts.astype(jnp.float32), axis=0)
    misfit = (weight * (picked - value)).astype(jnp.bfloat16)
    misfit = jnp.broadcast_to(misfit[None], (devices, tile, 128))
    misfit = lax.all_to_all(misfit, both, split_axis=0, concat_axis=0, tiled=True)
    misfit = misfit.reshape(part.shape)
    return backward(order_map, where, e_all, four, misfit, legendre, control, loc_spectrum)


def solution(mesh):
    rows = P("wide", None)
    return jax.shard_map(
        body,
        mesh=mesh,
        in_specs=(
            P("wide", None, None, "narrow"),
            P("wide", None, None),
            rows,
            P("wide", "narrow", None),
            P(),
            rows,
            rows,
            rows,
            rows,
        ),
        out_specs=P("wide", None, None, "narrow"),
        check_vma=False,
    )
```

```python
import jax
import jax.numpy as jnp
from jax import lax
from jax.experimental import pallas as pl
from jax.experimental.pallas import tpu as pltpu
from jax.sharding import PartitionSpec as P


LEVELS = 8
ROWS = 16
PLANES = 18
PICK = 4
ORDERS = 2
BLOCKS = 2
PITCH = 33
SIN = (6.2831851595779975, -41.34165492085311, 81.60099762205961, -76.54964290998956, 39.53570242643394)
COS = (0.9999999532360554, -19.739171315085017, 64.93458093602055, -85.24007915837501, 56.24034662339592)
HALF_SIN = tuple(2**0.5 * c / 2 ** (2 * i + 1) for i, c in enumerate(SIN))
HALF_COS = tuple(-(2**0.5) * c / 4**i for i, c in enumerate(COS))


def params(mib):
    return pltpu.CompilerParams(vmem_limit_bytes=mib * 2**20)


def in_hbm(x):
    return pltpu.with_memory_space_constraint(x, pltpu.HBM)


def horner(coefs, x):
    total = jnp.full_like(x, coefs[-1])
    for c in coefs[-2::-1]:
        total = total * x + c
    return total


def pick_kernel(level_ref, lon_ref, ens_ref, out_ref):
    b0 = pl.program_id(0) * PICK

    @pl.when(b0 == 0)
    def _():
        lon = lon_ref[...]
        out_ref[16] = (lon >> 3).astype(jnp.float32).astype(jnp.bfloat16)
        out_ref[17] = ((lon & 7) * LEVELS + level_ref[...]).astype(jnp.float32).astype(jnp.bfloat16)

    members, nobs = out_ref.shape[1], out_ref.shape[2]
    lons = ens_ref.shape[2]
    step = 256
    place = lax.broadcasted_iota(jnp.int32, (step, nobs), 0).astype(jnp.float32)
    place = place.astype(jnp.bfloat16)
    for k in range(PICK):
        lon = lon_ref[pl.ds(b0 + k, 1), :]
        level = level_ref[pl.ds(b0 + k, 1), :]
        onehot = []
        for s in range(0, lons, step):
            away = jnp.broadcast_to((lon - s).astype(jnp.float32), (16, nobs)).astype(jnp.bfloat16)
            away = jnp.concatenate([away] * (step // 16), axis=0)
            onehot.append(jnp.where(place == away, jnp.bfloat16(1), jnp.bfloat16(0)))
        total = jnp.dot(
            ens_ref[k], jnp.concatenate(onehot, axis=0), preferred_element_type=jnp.float32
        )
        mine = lax.broadcasted_iota(jnp.int32, (LEVELS, nobs), 0) == level
        total = jnp.where(mine[None], total.reshape(members, LEVELS, nobs), 0.0)
        out_ref[b0 + k] = jnp.sum(total, axis=1).astype(jnp.bfloat16)


def pick(obs_level, obs_lon, ensemble):
    rows, width, lons = ensemble.shape
    nobs = obs_lon.shape[1]
    whole = pl.BlockSpec((rows, nobs), lambda b: (0, 0))
    return pl.pallas_call(
        pick_kernel,
        grid=(rows // PICK,),
        in_specs=[whole, whole, pl.BlockSpec((PICK, width, lons), lambda b: (b, 0, 0))],
        out_specs=pl.BlockSpec((PLANES, rows, nobs), lambda b: (0, 0, 0)),
        out_shape=jax.ShapeDtypeStruct((PLANES, rows, nobs), jnp.bfloat16),
        compiler_params=params(12),
        name="pick",
    )(in_hbm(obs_level), in_hbm(obs_lon), in_hbm(ensemble))


def order_of(order_ref, place_ref, m):
    return order_ref[((place_ref[0] * 4 + place_ref[1]) * 2 + place_ref[2]) * ROWS + m]


def column(loc_ref, m, order):
    row = loc_ref[pl.ds(m, 1), :]
    row = jnp.where(order == 0, row, row * 2.0)
    return jnp.broadcast_to(row, (128, row.shape[1])).T


def legendre_kernel(order_ref, place_ref, leg_ref, control_ref, loc_ref, out_ref, acc_ref):
    step = pl.program_id(0)
    lats = out_ref.shape[0]
    width = control_ref.shape[3]
    for k in range(ORDERS):
        m = step * ORDERS + k
        loc = column(loc_ref, m, order_of(order_ref, place_ref, m))
        scaled = [
            (control_ref[k, c].astype(jnp.float32) * loc).astype(jnp.bfloat16) for c in range(2)
        ]
        got = lax.dot_general(
            leg_ref[k],
            jnp.concatenate(scaled, axis=1),
            (((0,), (0,)), ((), ())),
            preferred_element_type=jnp.float32,
        )
        for c in range(2):
            acc_ref[pl.ds(c * ROWS + m, lats, stride=PITCH), :] = got[
                :, c * width : (c + 1) * width
            ]

    @pl.when(step == pl.num_programs(0) - 1)
    def _():
        def move(i, carry):
            for k in range(16):
                b = i * 16 + k
                out_ref[b] = acc_ref[pl.ds(b * PITCH, 2 * ROWS), :].astype(jnp.bfloat16)
            return carry

        lax.fori_loop(0, lats // 16, move, 0)


def legendre_forward(order_map, where, legendre, control, loc):
    slots, _, degs, width = control.shape
    lats = legendre.shape[2]
    return pl.pallas_call(
        legendre_kernel,
        grid_spec=pltpu.PrefetchScalarGridSpec(
            num_scalar_prefetch=2,
            grid=(slots // ORDERS,),
            in_specs=[
                pl.BlockSpec((ORDERS, degs, lats), lambda m, *_: (m, 0, 0)),
                pl.BlockSpec((ORDERS, 2, degs, width), lambda m, *_: (m, 0, 0, 0)),
                pl.BlockSpec((slots, degs), lambda m, *_: (0, 0)),
            ],
            out_specs=pl.BlockSpec((lats, 2 * slots, width), lambda m, *_: (0, 0, 0)),
            scratch_shapes=[pltpu.VMEM((lats * PITCH, width), jnp.float32)],
        ),
        out_shape=jax.ShapeDtypeStruct((lats, 2 * slots, width), jnp.bfloat16),
        compiler_params=params(22),
        cost_estimate=pl.CostEstimate(
            flops=2 * slots * degs * lats * 2 * width, bytes_accessed=16 * 2**20, transcendentals=0
        ),
        name="legendre_forward",
    )(order_map, where, in_hbm(legendre), in_hbm(control), in_hbm(loc))


def forward_kernel(order_ref, place_ref, e_ref, coeff_ref, *rest):
    part_ref, four_ref, keep_ref, lon_ref, lev_ref, ens_ref, sum_ref, turn_ref = rest[-8:]
    hi = e_ref[0, 16].astype(jnp.float32)
    lo = e_ref[0, 17].astype(jnp.float32)
    low = jnp.floor(lo * (1.0 / LEVELS))
    lon_ref[...] = hi * 8.0 + low
    lev_ref[...] = lo - low * LEVELS
    keep_ref[0] = e_ref[0]
    members, nobs = e_ref.shape[2], e_ref.shape[3]
    ens_ref[...] = e_ref[0, :ROWS].astype(jnp.float32)

    @pl.when(pl.program_id(0) == 0)
    def _():
        row = lax.broadcasted_iota(jnp.int32, turn_ref.shape, 0)
        order = jnp.zeros(turn_ref.shape, jnp.float32)
        for m in range(ROWS):
            order = jnp.where(
                row == m, order_of(order_ref, place_ref, m).astype(jnp.float32), order
            )
        turn_ref[...] = order * (1.0 / 1024.0)

    turn = turn_ref[...]
    grid_level = lax.broadcasted_iota(jnp.int32, (LEVELS, nobs), 0).astype(jnp.float32)

    def one(b):
        turns = turn * lon_ref[pl.ds(b, 1), :]
        frac = turns - jnp.floor(turns + 0.5)
        square = frac * frac
        sine = frac * horner(HALF_SIN, square)
        cosine = horner(HALF_COS, square)
        four = jnp.concatenate(
            [(1.0 - sine * sine).astype(jnp.bfloat16), (sine * cosine).astype(jnp.bfloat16)],
            axis=0,
        )
        four_ref[0, b] = four
        field = lax.dot_general(
            coeff_ref[b], four, (((0,), (0,)), ((), ())), preferred_element_type=jnp.float32
        )
        total = None
        for k in range(members):
            ens = ens_ref[b, k : k + 1]
            term = field[k * LEVELS : (k + 1) * LEVELS] * ens
            total = term if total is None else total + term
        mine = grid_level == lev_ref[pl.ds(b, 1), :]
        total = jnp.sum(jnp.where(mine, total, 0.0), axis=0, keepdims=True)
        for lane in range(0, nobs, 128):
            sum_ref[pl.ds((b * nobs + lane) // 128, 1), :] = total[:, lane : lane + 128]

    for b in range(ROWS):
        one(b)
    part_ref[...] = sum_ref[...].astype(jnp.bfloat16)


def forward(order_map, where, plane, far, e, coeff, before):
    n = e.shape[0]
    lats, modes, width = coeff.shape
    nobs = e.shape[3]
    blocks = lats // ROWS
    lanes = nobs // 128

    def block(i, place):
        turn = (far - i) * place[3]
        z, y = place[0] - far + turn, place[1] - i - turn
        return (z & 3) * 8 + (y & 3) * 2 + ((place[2] + plane) & 1)

    e_spec = lambda f: pl.BlockSpec((1, PLANES, ROWS, nobs), f)
    at_block = lambda i, _, place: (block(i, place), 0, 0, 0)
    out_shape = (
        jax.ShapeDtypeStruct((lats * lanes, 128), jnp.bfloat16),
        jax.ShapeDtypeStruct((blocks, ROWS, modes, nobs), jnp.bfloat16),
        jax.ShapeDtypeStruct((blocks, PLANES, ROWS, nobs), jnp.bfloat16),
    )
    passed = () if before is None else tuple(before)
    return pl.pallas_call(
        forward_kernel,
        grid_spec=pltpu.PrefetchScalarGridSpec(
            num_scalar_prefetch=2,
            grid=(n,),
            in_specs=[
                e_spec(lambda i, _, place: (i, 0, 0, 0)),
                pl.BlockSpec((ROWS, modes, width), lambda i, _, place: (block(i, place), 0, 0)),
            ]
            + [pl.BlockSpec(memory_space=pl.ANY)] * len(passed),
            out_specs=(
                pl.BlockSpec((ROWS * lanes, 128), lambda i, _, place: (block(i, place), 0)),
                pl.BlockSpec((1, ROWS, modes, nobs), at_block),
                e_spec(at_block),
            ),
            scratch_shapes=[
                pltpu.VMEM((ROWS, nobs), jnp.float32),
                pltpu.VMEM((ROWS, nobs), jnp.float32),
                pltpu.VMEM((ROWS, ROWS, nobs), jnp.float32),
                pltpu.VMEM((ROWS * lanes, 128), jnp.float32),
                pltpu.VMEM((ROWS, nobs), jnp.float32),
            ],
        ),
        out_shape=out_shape,
        input_output_aliases={4 + i: i for i in range(len(passed))},
        compiler_params=params(6),
        cost_estimate=pl.CostEstimate(
            flops=n * 6 * 10**8, bytes_accessed=n * 2**19, transcendentals=0
        ),
        name="observe",
    )(order_map, where, e, coeff, *passed)


def backward_kernel(
    order_ref, place_ref, e_ref, four_ref, misfit_ref, leg_ref, control_ref, loc_ref, out_ref,
    back_ref, lev_ref, ens_ref, misfit32_ref,
):
    step = pl.program_id(0)
    nobs = e_ref.shape[3]
    members = e_ref.shape[2]
    modes = four_ref.shape[2]
    lats = back_ref.shape[0] // PITCH
    width = control_ref.shape[3]
    steps = lats // (ROWS * BLOCKS)

    @pl.when(step < steps)
    def _():
        misfit32_ref[...] = misfit_ref[...].astype(jnp.float32)
        grid_level = lax.broadcasted_iota(jnp.int32, (LEVELS, nobs), 0).astype(jnp.float32)
        for g in range(BLOCKS):
            lo = e_ref[g, 17].astype(jnp.float32)
            lev_ref[g] = lo - jnp.floor(lo * (1.0 / LEVELS)) * LEVELS
            for b in range(ROWS):
                row = (g * ROWS + b) * nobs // 128
                misfit = jnp.concatenate(
                    [
                        jnp.broadcast_to(misfit32_ref[row + lane : row + lane + 1], (members, 128))
                        for lane in range(nobs // 128)
                    ],
                    axis=1,
                )
                ens_ref[g, b] = e_ref[g, b].astype(jnp.float32) * misfit
            for b in range(ROWS):
                mine = grid_level == lev_ref[g, b : b + 1]
                spread = [
                    jnp.where(mine, ens_ref[g, b, k : k + 1], 0.0) for k in range(members)
                ]
                lat = (step * BLOCKS + g) * ROWS + b
                back_ref[pl.ds(lat * PITCH, modes), :] = lax.dot_general(
                    four_ref[g, b],
                    jnp.concatenate(spread, axis=0).astype(jnp.bfloat16),
                    (((1,), (1,)), ((), ())),
                    preferred_element_type=jnp.float32,
                )

    @pl.when(step >= steps)
    def _():
        for k in range(ORDERS):
            m = (step - steps) * ORDERS + k
            pieces = [
                back_ref[pl.ds(c * ROWS + m, lats, stride=PITCH), :].astype(jnp.bfloat16)
                for c in range(2)
            ]
            got = jnp.dot(
                leg_ref[k], jnp.concatenate(pieces, axis=1), preferred_element_type=jnp.float32
            )
            loc = column(loc_ref, m, order_of(order_ref, place_ref, m))
            for c in range(2):
                out_ref[k, c] = (
                    control_ref[k, c].astype(jnp.float32)
                    + loc * got[:, c * width : (c + 1) * width]
                )


def backward(order_map, where, e, four, misfit, legendre, control, loc):
    blocks, _, _, nobs = e.shape
    modes = four.shape[2]
    slots, _, degs, width = control.shape
    lats = legendre.shape[2]
    lanes = nobs // 128
    steps = blocks // BLOCKS
    first = lambda s: jnp.minimum(s, steps - 1)
    second = lambda s: jnp.maximum(s - steps, 0)
    per_slot = pl.BlockSpec((ORDERS, 2, degs, width), lambda s, *_: (second(s), 0, 0, 0))
    return pl.pallas_call(
        backward_kernel,
        grid_spec=pltpu.PrefetchScalarGridSpec(
            num_scalar_prefetch=2,
            grid=(steps + slots // ORDERS,),
            in_specs=[
                pl.BlockSpec((BLOCKS, PLANES, ROWS, nobs), lambda s, *_: (first(s), 0, 0, 0)),
                pl.BlockSpec((BLOCKS, ROWS, modes, nobs), lambda s, *_: (first(s), 0, 0, 0)),
                pl.BlockSpec((BLOCKS * ROWS * lanes, 128), lambda s, *_: (first(s), 0)),
                pl.BlockSpec((ORDERS, degs, lats), lambda s, *_: (second(s), 0, 0)),
                per_slot,
                pl.BlockSpec((slots, degs), lambda s, *_: (0, 0)),
            ],
            out_specs=per_slot,
            scratch_shapes=[
                pltpu.VMEM((lats * PITCH, width), jnp.float32),
                pltpu.VMEM((BLOCKS, ROWS, nobs), jnp.float32),
                pltpu.VMEM((BLOCKS, ROWS, ROWS, nobs), jnp.float32),
                pltpu.VMEM((BLOCKS * ROWS * lanes, 128), jnp.float32),
            ],
        ),
        out_shape=jax.ShapeDtypeStruct(control.shape, jnp.float32),
        compiler_params=params(24),
        name="adjoint",
    )(order_map, where, e, four, misfit, in_hbm(legendre), in_hbm(control), in_hbm(loc))


def send(x, distance, stage):
    pairs = []
    for w in range(32):
        for n in range(4):
            z, y, h = w // 8, w // 2 % 4, w % 2
            if stage == "hop":
                h = (h + distance) % 2
            elif (stage == "near") == (n % 2 == 0):
                y = (y + distance) % 4
            else:
                z = (z + distance) % 4
            pairs.append((w * 4 + n, (z * 8 + y * 2 + h) * 4 + n))
    return lax.ppermute(x, ("wide", "narrow"), pairs)


def gather(own):
    ring = (1, 3, 2)
    near = {k: send(own, k, "near") for k in ring}
    near = jnp.concatenate([own] + [near[k] for k in (1, 2, 3)], axis=0)
    other = send(near, 1, "hop")
    far = [(0, k, send(near, k, "far")) for k in ring]
    across = [(1, k, send(other, k, "far")) for k in ring]
    return [(0, 0, near)] + far + [(1, 0, other)] + across


def body(
    control, legendre, loc_spectrum, ensemble, order_map, obs_level, obs_lon, obs_value, obs_weight
):
    nobs = obs_lon.shape[1]
    both = ("wide", "narrow")
    devices = lax.axis_size(both)
    mine = obs_lon.shape[0] * lax.axis_size("wide") // devices
    tile = mine * nobs // 128
    w = lax.axis_index("wide")
    n = lax.axis_index("narrow")
    where = jnp.stack([w >> 3, (w >> 1) & 3, w & 1, n & 1]).astype(jnp.int32)
    own = pick(obs_level, obs_lon, ensemble)

    blocks = gather(own)

    coeff = legendre_forward(order_map, where, legendre, control, loc_spectrum)
    state = None
    for plane, far, e in blocks:
        e = e.reshape(-1, PLANES, ROWS, nobs)
        state = forward(order_map, where, plane, far, e, coeff, state)
    part, four, e_all = state

    value = lax.dynamic_slice_in_dim(obs_value, n * mine, mine, 0).reshape(tile, 128)
    weight = lax.dynamic_slice_in_dim(obs_weight, n * mine, mine, 0).reshape(tile, 128)
    part, value, weight = lax.optimization_barrier((part, value, weight))
    parts = lax.all_to_all(
        part.reshape(devices, tile, 128), both, split_axis=0, concat_axis=0, tiled=True
    )
    picked = jnp.sum(parts.astype(jnp.float32), axis=0)
    misfit = (weight * (picked - value)).astype(jnp.bfloat16)
    misfit = jnp.broadcast_to(misfit[None], (devices, tile, 128))
    misfit = lax.all_to_all(misfit, both, split_axis=0, concat_axis=0, tiled=True)
    misfit = misfit.reshape(part.shape)
    return backward(order_map, where, e_all, four, misfit, legendre, control, loc_spectrum)


def solution(mesh):
    rows = P("wide", None)
    return jax.shard_map(
        body,
        mesh=mesh,
        in_specs=(
            P("wide", None, None, "narrow"),
            P("wide", None, None),
            rows,
            P("wide", "narrow", None),
            P(),
            rows,
            rows,
            rows,
            rows,
        ),
        out_specs=P("wide", None, None, "narrow"),
        check_vma=False,
    )
```

```python
import jax
import jax.numpy as jnp
from jax import lax
from jax.experimental import pallas as pl
from jax.experimental.pallas import tpu as pltpu
from jax.sharding import PartitionSpec as P


LEVELS = 8
ROWS = 16
PLANES = 18
PICK = 4
ORDERS = 2
BLOCKS = 2
PITCH = 33
SIN = (6.2831851595779975, -41.34165492085311, 81.60099762205961, -76.54964290998956, 39.53570242643394)
COS = (0.9999999532360554, -19.739171315085017, 64.93458093602055, -85.24007915837501, 56.24034662339592)
HALF_SIN = tuple(2**0.5 * c / 2 ** (2 * i + 1) for i, c in enumerate(SIN))
HALF_COS = tuple(-(2**0.5) * c / 4**i for i, c in enumerate(COS))


def params(mib):
    return pltpu.CompilerParams(vmem_limit_bytes=mib * 2**20)


def in_hbm(x):
    return pltpu.with_memory_space_constraint(x, pltpu.HBM)


def horner(coefs, x):
    total = jnp.full_like(x, coefs[-1])
    for c in coefs[-2::-1]:
        total = total * x + c
    return total


def pick_kernel(level_ref, lon_ref, ens_ref, out_ref):
    b0 = pl.program_id(0) * PICK

    @pl.when(b0 == 0)
    def _():
        lon = lon_ref[...]
        out_ref[16] = (lon >> 3).astype(jnp.float32).astype(jnp.bfloat16)
        out_ref[17] = ((lon & 7) * LEVELS + level_ref[...]).astype(jnp.float32).astype(jnp.bfloat16)

    members, nobs = out_ref.shape[1], out_ref.shape[2]
    lons = ens_ref.shape[2]
    step = 256
    place = lax.broadcasted_iota(jnp.int32, (step, nobs), 0).astype(jnp.float32)
    place = place.astype(jnp.bfloat16)
    for k in range(PICK):
        lon = lon_ref[pl.ds(b0 + k, 1), :]
        level = level_ref[pl.ds(b0 + k, 1), :]
        onehot = []
        for s in range(0, lons, step):
            away = jnp.broadcast_to((lon - s).astype(jnp.float32), (16, nobs)).astype(jnp.bfloat16)
            away = jnp.concatenate([away] * (step // 16), axis=0)
            onehot.append(jnp.where(place == away, jnp.bfloat16(1), jnp.bfloat16(0)))
        total = jnp.dot(
            ens_ref[k], jnp.concatenate(onehot, axis=0), preferred_element_type=jnp.float32
        )
        mine = lax.broadcasted_iota(jnp.int32, (LEVELS, nobs), 0) == level
        total = jnp.where(mine[None], total.reshape(members, LEVELS, nobs), 0.0)
        out_ref[b0 + k] = jnp.sum(total, axis=1).astype(jnp.bfloat16)


def pick(obs_level, obs_lon, ensemble):
    rows, width, lons = ensemble.shape
    nobs = obs_lon.shape[1]
    whole = pl.BlockSpec((rows, nobs), lambda b: (0, 0))
    return pl.pallas_call(
        pick_kernel,
        grid=(rows // PICK,),
        in_specs=[whole, whole, pl.BlockSpec((PICK, width, lons), lambda b: (b, 0, 0))],
        out_specs=pl.BlockSpec((PLANES, rows, nobs), lambda b: (0, 0, 0)),
        out_shape=jax.ShapeDtypeStruct((PLANES, rows, nobs), jnp.bfloat16),
        compiler_params=params(12),
        name="pick",
    )(in_hbm(obs_level), in_hbm(obs_lon), in_hbm(ensemble))


def order_of(order_ref, place_ref, m):
    return order_ref[((place_ref[0] * 4 + place_ref[1]) * 2 + place_ref[2]) * ROWS + m]


def column(loc_ref, m, order):
    row = loc_ref[pl.ds(m, 1), :]
    row = jnp.where(order == 0, row, row * 2.0)
    return jnp.broadcast_to(row, (128, row.shape[1])).T


def legendre_kernel(order_ref, place_ref, leg_ref, control_ref, loc_ref, out_ref, acc_ref):
    step = pl.program_id(0)
    lats = out_ref.shape[0]
    width = control_ref.shape[3]
    for k in range(ORDERS):
        m = step * ORDERS + k
        loc = column(loc_ref, m, order_of(order_ref, place_ref, m))
        scaled = [
            (control_ref[k, c].astype(jnp.float32) * loc).astype(jnp.bfloat16) for c in range(2)
        ]
        got = lax.dot_general(
            leg_ref[k],
            jnp.concatenate(scaled, axis=1),
            (((0,), (0,)), ((), ())),
            preferred_element_type=jnp.float32,
        )
        for c in range(2):
            acc_ref[pl.ds(c * ROWS + m, lats, stride=PITCH), :] = got[
                :, c * width : (c + 1) * width
            ]

    @pl.when(step == pl.num_programs(0) - 1)
    def _():
        def move(i, carry):
            for k in range(16):
                b = i * 16 + k
                out_ref[b] = acc_ref[pl.ds(b * PITCH, 2 * ROWS), :].astype(jnp.bfloat16)
            return carry

        lax.fori_loop(0, lats // 16, move, 0)


def legendre_forward(order_map, where, legendre, control, loc):
    slots, _, degs, width = control.shape
    lats = legendre.shape[2]
    return pl.pallas_call(
        legendre_kernel,
        grid_spec=pltpu.PrefetchScalarGridSpec(
            num_scalar_prefetch=2,
            grid=(slots // ORDERS,),
            in_specs=[
                pl.BlockSpec((ORDERS, degs, lats), lambda m, *_: (m, 0, 0)),
                pl.BlockSpec((ORDERS, 2, degs, width), lambda m, *_: (m, 0, 0, 0)),
                pl.BlockSpec((slots, degs), lambda m, *_: (0, 0)),
            ],
            out_specs=pl.BlockSpec((lats, 2 * slots, width), lambda m, *_: (0, 0, 0)),
            scratch_shapes=[pltpu.VMEM((lats * PITCH, width), jnp.float32)],
        ),
        out_shape=jax.ShapeDtypeStruct((lats, 2 * slots, width), jnp.bfloat16),
        compiler_params=params(22),
        cost_estimate=pl.CostEstimate(
            flops=2 * slots * degs * lats * 2 * width, bytes_accessed=16 * 2**20, transcendentals=0
        ),
        name="legendre_forward",
    )(order_map, where, in_hbm(legendre), in_hbm(control), in_hbm(loc))


def forward_kernel(order_ref, place_ref, e0_ref, e1_ref, e2_ref, e3_ref, coeff_ref, *rest):
    part_ref, four_ref, keep_ref, lon_ref, lev_ref, ens_ref, sum_ref, turn_ref = rest[-8:]
    part = pl.program_id(0) >> 2
    for q, ref in enumerate((e0_ref, e1_ref, e2_ref, e3_ref)):

        @pl.when(part == q)
        def _(ref=ref):
            keep_ref[...] = ref[...]

    hi = keep_ref[0, 16].astype(jnp.float32)
    lo = keep_ref[0, 17].astype(jnp.float32)
    low = jnp.floor(lo * (1.0 / LEVELS))
    lon_ref[...] = hi * 8.0 + low
    lev_ref[...] = lo - low * LEVELS
    members, nobs = keep_ref.shape[2], keep_ref.shape[3]
    ens_ref[...] = keep_ref[0, :ROWS].astype(jnp.float32)

    @pl.when(pl.program_id(0) == 0)
    def _():
        row = lax.broadcasted_iota(jnp.int32, turn_ref.shape, 0)
        order = jnp.zeros(turn_ref.shape, jnp.float32)
        for m in range(ROWS):
            order = jnp.where(
                row == m, order_of(order_ref, place_ref, m).astype(jnp.float32), order
            )
        turn_ref[...] = order * (1.0 / 1024.0)

    turn = turn_ref[...]
    grid_level = lax.broadcasted_iota(jnp.int32, (LEVELS, nobs), 0).astype(jnp.float32)

    def one(b):
        turns = turn * lon_ref[pl.ds(b, 1), :]
        frac = turns - jnp.floor(turns + 0.5)
        square = frac * frac
        sine = frac * horner(HALF_SIN, square)
        cosine = horner(HALF_COS, square)
        four = jnp.concatenate(
            [(1.0 - sine * sine).astype(jnp.bfloat16), (sine * cosine).astype(jnp.bfloat16)],
            axis=0,
        )
        four_ref[0, b] = four
        field = lax.dot_general(
            coeff_ref[b], four, (((0,), (0,)), ((), ())), preferred_element_type=jnp.float32
        )
        total = None
        for k in range(members):
            ens = ens_ref[b, k : k + 1]
            term = field[k * LEVELS : (k + 1) * LEVELS] * ens
            total = term if total is None else total + term
        mine = grid_level == lev_ref[pl.ds(b, 1), :]
        total = jnp.sum(jnp.where(mine, total, 0.0), axis=0, keepdims=True)
        for lane in range(0, nobs, 128):
            sum_ref[pl.ds((b * nobs + lane) // 128, 1), :] = total[:, lane : lane + 128]

    for b in range(ROWS):
        one(b)
    part_ref[...] = sum_ref[...].astype(jnp.bfloat16)


def forward(order_map, where, plane, arrays, coeff, before):
    lats, modes, width = coeff.shape
    nobs = arrays[0].shape[3]
    blocks = lats // ROWS
    lanes = nobs // 128
    n = 4 * len(arrays)

    def block(i, place):
        near, part = i & 3, i >> 2
        far = part ^ (part >> 1)
        turn = (far - near) * place[3]
        z, y = place[0] - far + turn, place[1] - near - turn
        return (z & 3) * 8 + (y & 3) * 2 + ((place[2] + plane) & 1)

    e_spec = lambda f: pl.BlockSpec((1, PLANES, ROWS, nobs), f)
    at_block = lambda i, _, place: (block(i, place), 0, 0, 0)
    out_shape = (
        jax.ShapeDtypeStruct((lats * lanes, 128), jnp.bfloat16),
        jax.ShapeDtypeStruct((blocks, ROWS, modes, nobs), jnp.bfloat16),
        jax.ShapeDtypeStruct((blocks, PLANES, ROWS, nobs), jnp.bfloat16),
    )
    passed = () if before is None else tuple(before)
    return pl.pallas_call(
        forward_kernel,
        grid_spec=pltpu.PrefetchScalarGridSpec(
            num_scalar_prefetch=2,
            grid=(n,),
            in_specs=[
                *[e_spec(lambda i, *_, q=q: (jnp.clip(i - 4 * q, 0, 3), 0, 0, 0)) for q in range(4)],
                pl.BlockSpec((ROWS, modes, width), lambda i, _, place: (block(i, place), 0, 0)),
            ]
            + [pl.BlockSpec(memory_space=pl.ANY)] * len(passed),
            out_specs=(
                pl.BlockSpec((ROWS * lanes, 128), lambda i, _, place: (block(i, place), 0)),
                pl.BlockSpec((1, ROWS, modes, nobs), at_block),
                e_spec(at_block),
            ),
            scratch_shapes=[
                pltpu.VMEM((ROWS, nobs), jnp.float32),
                pltpu.VMEM((ROWS, nobs), jnp.float32),
                pltpu.VMEM((ROWS, ROWS, nobs), jnp.float32),
                pltpu.VMEM((ROWS * lanes, 128), jnp.float32),
                pltpu.VMEM((ROWS, nobs), jnp.float32),
            ],
        ),
        out_shape=out_shape,
        input_output_aliases={7 + i: i for i in range(len(passed))},
        compiler_params=params(8),
        cost_estimate=pl.CostEstimate(
            flops=n * 6 * 10**8, bytes_accessed=n * 2**19, transcendentals=0
        ),
        name="observe",
    )(order_map, where, *arrays, coeff, *passed)


def backward_kernel(
    order_ref, place_ref, e_ref, four_ref, misfit_ref, leg_ref, control_ref, loc_ref, out_ref,
    back_ref, lev_ref, ens_ref, misfit32_ref,
):
    step = pl.program_id(0)
    nobs = e_ref.shape[3]
    members = e_ref.shape[2]
    modes = four_ref.shape[2]
    lats = back_ref.shape[0] // PITCH
    width = control_ref.shape[3]
    steps = lats // (ROWS * BLOCKS)

    @pl.when(step < steps)
    def _():
        misfit32_ref[...] = misfit_ref[...].astype(jnp.float32)
        grid_level = lax.broadcasted_iota(jnp.int32, (LEVELS, nobs), 0).astype(jnp.float32)
        for g in range(BLOCKS):
            lo = e_ref[g, 17].astype(jnp.float32)
            lev_ref[g] = lo - jnp.floor(lo * (1.0 / LEVELS)) * LEVELS
            for b in range(ROWS):
                row = (g * ROWS + b) * nobs // 128
                misfit = jnp.concatenate(
                    [
                        jnp.broadcast_to(misfit32_ref[row + lane : row + lane + 1], (members, 128))
                        for lane in range(nobs // 128)
                    ],
                    axis=1,
                )
                ens_ref[g, b] = e_ref[g, b].astype(jnp.float32) * misfit
            for b in range(ROWS):
                mine = grid_level == lev_ref[g, b : b + 1]
                spread = [
                    jnp.where(mine, ens_ref[g, b, k : k + 1], 0.0) for k in range(members)
                ]
                lat = (step * BLOCKS + g) * ROWS + b
                back_ref[pl.ds(lat * PITCH, modes), :] = lax.dot_general(
                    four_ref[g, b],
                    jnp.concatenate(spread, axis=0).astype(jnp.bfloat16),
                    (((1,), (1,)), ((), ())),
                    preferred_element_type=jnp.float32,
                )

    @pl.when(step >= steps)
    def _():
        for k in range(ORDERS):
            m = (step - steps) * ORDERS + k
            pieces = [
                back_ref[pl.ds(c * ROWS + m, lats, stride=PITCH), :].astype(jnp.bfloat16)
                for c in range(2)
            ]
            got = jnp.dot(
                leg_ref[k], jnp.concatenate(pieces, axis=1), preferred_element_type=jnp.float32
            )
            loc = column(loc_ref, m, order_of(order_ref, place_ref, m))
            for c in range(2):
                out_ref[k, c] = (
                    control_ref[k, c].astype(jnp.float32)
                    + loc * got[:, c * width : (c + 1) * width]
                )


def backward(order_map, where, e, four, misfit, legendre, control, loc):
    blocks, _, _, nobs = e.shape
    modes = four.shape[2]
    slots, _, degs, width = control.shape
    lats = legendre.shape[2]
    lanes = nobs // 128
    steps = blocks // BLOCKS
    first = lambda s: jnp.minimum(s, steps - 1)
    second = lambda s: jnp.maximum(s - steps, 0)
    per_slot = pl.BlockSpec((ORDERS, 2, degs, width), lambda s, *_: (second(s), 0, 0, 0))
    return pl.pallas_call(
        backward_kernel,
        grid_spec=pltpu.PrefetchScalarGridSpec(
            num_scalar_prefetch=2,
            grid=(steps + slots // ORDERS,),
            in_specs=[
                pl.BlockSpec((BLOCKS, PLANES, ROWS, nobs), lambda s, *_: (first(s), 0, 0, 0)),
                pl.BlockSpec((BLOCKS, ROWS, modes, nobs), lambda s, *_: (first(s), 0, 0, 0)),
                pl.BlockSpec((BLOCKS * ROWS * lanes, 128), lambda s, *_: (first(s), 0)),
                pl.BlockSpec((ORDERS, degs, lats), lambda s, *_: (second(s), 0, 0)),
                per_slot,
                pl.BlockSpec((slots, degs), lambda s, *_: (0, 0)),
            ],
            out_specs=per_slot,
            scratch_shapes=[
                pltpu.VMEM((lats * PITCH, width), jnp.float32),
                pltpu.VMEM((BLOCKS, ROWS, nobs), jnp.float32),
                pltpu.VMEM((BLOCKS, ROWS, ROWS, nobs), jnp.float32),
                pltpu.VMEM((BLOCKS * ROWS * lanes, 128), jnp.float32),
            ],
        ),
        out_shape=jax.ShapeDtypeStruct(control.shape, jnp.float32),
        compiler_params=params(24),
        name="adjoint",
    )(order_map, where, e, four, misfit, legendre, control, in_hbm(loc))


def send(x, distance, stage):
    pairs = []
    for w in range(32):
        for n in range(4):
            z, y, h = w // 8, w // 2 % 4, w % 2
            if stage == "hop":
                h = (h + distance) % 2
            elif (stage == "near") == (n % 2 == 0):
                y = (y + distance) % 4
            else:
                z = (z + distance) % 4
            pairs.append((w * 4 + n, (z * 8 + y * 2 + h) * 4 + n))
    return lax.ppermute(x, ("wide", "narrow"), pairs)


def gather(own):
    ring = (1, 3, 2)
    near = {k: send(own, k, "near") for k in ring}
    near = jnp.concatenate([own] + [near[k] for k in (1, 2, 3)], axis=0)
    other = send(near, 1, "hop")
    far = [send(near, k, "far") for k in ring]
    across = [send(other, k, "far") for k in ring]
    return [near] + far, [other] + across


def body(
    control, legendre, loc_spectrum, ensemble, order_map, obs_level, obs_lon, obs_value, obs_weight
):
    nobs = obs_lon.shape[1]
    both = ("wide", "narrow")
    devices = lax.axis_size(both)
    mine = obs_lon.shape[0] * lax.axis_size("wide") // devices
    tile = mine * nobs // 128
    w = lax.axis_index("wide")
    n = lax.axis_index("narrow")
    where = jnp.stack([w >> 3, (w >> 1) & 3, w & 1, n & 1]).astype(jnp.int32)
    own = pick(obs_level, obs_lon, ensemble)

    planes = gather(own)

    coeff = legendre_forward(order_map, where, legendre, control, loc_spectrum)
    state = None
    for plane, arrays in enumerate(planes):
        arrays = [e.reshape(-1, PLANES, ROWS, nobs) for e in arrays]
        state = forward(order_map, where, plane, arrays, coeff, state)
    part, four, e_all = state

    value = lax.dynamic_slice_in_dim(obs_value, n * mine, mine, 0).reshape(tile, 128)
    weight = lax.dynamic_slice_in_dim(obs_weight, n * mine, mine, 0).reshape(tile, 128)
    part, value, weight = lax.optimization_barrier((part, value, weight))
    parts = lax.all_to_all(
        part.reshape(devices, tile, 128), both, split_axis=0, concat_axis=0, tiled=True
    )
    picked = jnp.sum(parts.astype(jnp.float32), axis=0)
    misfit = (weight * (picked - value)).astype(jnp.bfloat16)
    misfit = jnp.broadcast_to(misfit[None], (devices, tile, 128))
    misfit = lax.all_to_all(misfit, both, split_axis=0, concat_axis=0, tiled=True)
    misfit = misfit.reshape(part.shape)
    return backward(order_map, where, e_all, four, misfit, legendre, control, loc_spectrum)


def solution(mesh):
    rows = P("wide", None)
    return jax.shard_map(
        body,
        mesh=mesh,
        in_specs=(
            P("wide", None, None, "narrow"),
            P("wide", None, None),
            rows,
            P("wide", "narrow", None),
            P(),
            rows,
            rows,
            rows,
            rows,
        ),
        out_specs=P("wide", None, None, "narrow"),
        check_vma=False,
    )
```
